128 devices in a mesh: row: 8 (over y, core), col: 16 (over z, x).
Axes of the slice: x: 4, y: 4, z: 4, core: 2. Of those that a mesh axis runs over, the one named last changes fastest.
Arguments:
- ancestor_inverse: float32 [12288, 12288], P('row', 'col')
- factor: bfloat16 [3, 12288, 512], P(None, ('row', 'col')), may hold values from -0.5 to 0.5
- coupling: float32 [3, 512, 512], replicated, may hold values from -0.25 to 0.25
- diagonal_inverse: float32 [3, 512, 512], replicated, may hold values from -6 to 6
- ancestors: int32 [3, 24], replicated, may hold values from -1 to 23, as said below
Outputs:
- block_columns: float32 [3, 12288, 512], P(None, ('row', 'col'))
- block_rows: float32 [3, 12288, 512], P(None, ('col', 'row'))
- node_blocks: float32 [3, 3, 512, 512], replicated
The draws below stay inside these ranges and needn't reach their ends.
Inputs may be any that keep to these rules, and one draw needn't show every extreme that they name: `ancestors`: row k lists the ancestor block rows of supernode k, blocks of 512 rows: distinct indices in increasing order, then -1 in the slots left. Every block is listed by some supernode.
All inputs are finite; a program needn't handle non-finite values.
Results may differ from the reference program's by a relative error of at most 0.0003.
Values may be sent and summed in bfloat16 or wider, within the bound.
A program may use at most 128 MiB of HBM per device.

```python
import math
import jax
import jax.numpy as jnp
from jax import lax

ORDER = 12288
SN = 512
NODES = 3
NBLK = 24
PAIRS = 3


def draw_ancestor_inverse(key, part):
    key_noise, key_diag = jax.random.split(jax.random.fold_in(key, 11))
    noise_draw = jax.random.normal(key_noise, (ORDER, ORDER), jnp.float32)
    symmetric = (noise_draw + noise_draw.T) * (0.5 / ORDER) ** 0.5
    diagonal = jnp.exp(jax.random.uniform(key_diag, (ORDER,), jnp.float32, math.log(0.2), 0.0))
    return symmetric + jnp.diag(diagonal)


def draw_ancestors(key, part):
    key_order, key_extra = jax.random.split(jax.random.fold_in(key, 7))
    shuffled = jax.random.permutation(key_order, NBLK).astype(jnp.int32)
    positions = jnp.arange(NBLK, dtype=jnp.int32)
    node_ids = jnp.arange(NODES, dtype=jnp.int32)
    lower_bound = NBLK * node_ids * (node_ids + 1) // (NODES * (NODES + 1))
    upper_bound = NBLK * (node_ids + 1) * (node_ids + 2) // (NODES * (NODES + 1))
    by_place = (positions[None, :] >= lower_bound[:, None]) & (positions[None, :] < upper_bound[:, None])
    primary = jnp.zeros((NODES, NBLK), jnp.bool_).at[:, shuffled].set(by_place)
    additions = jax.random.randint(key_extra, (NODES, NBLK), 0, 3) == 0
    member = primary | additions
    sort_keys = jnp.where(member, positions[None, :], NBLK + positions[None, :])
    ranked = jnp.sort(sort_keys, axis=1)
    return jnp.where(ranked < NBLK, ranked, -1).astype(jnp.int32)


def block_levels(key, shape, cuts, least, largest):
    loudness = 1.0
    for axis_at, blocks in cuts:
        heights = jax.random.uniform(jax.random.fold_in(jax.random.fold_in(key, 6), axis_at), (blocks,), jnp.float32, least / len(cuts), largest / len(cuts))
        loudness = loudness * jnp.repeat(jnp.exp(heights), shape[axis_at] // blocks).reshape((-1,) + (1,) * (len(shape) - 1 - axis_at))
    return loudness


def normal_values(rng, dims, width, reach, shards=(), held_as=jnp.bfloat16):
    drawn = width * jax.random.normal(rng, dims, jnp.float32)
    if shards:
        drawn = drawn * block_levels(rng, dims, shards, -0.22, 0.18)
    return jnp.clip(drawn, -reach, reach).astype(held_as)


def setup_inputs(seed: int = 0) -> dict:
    seeds = jax.random.split(jax.random.key(seed), 6)
    ancestor_inverse = draw_ancestor_inverse(jax.random.fold_in(seeds[5], 71), 0)
    factor = normal_values(seeds[1], (NODES, ORDER, SN), 0.0625, 0.5, ((1, 128),))
    coupling = normal_values(seeds[2], (PAIRS, SN, SN), SN ** -0.5, 0.25, (), jnp.float32)
    diagonal_inverse = normal_values(seeds[3], (NODES, SN, SN), 1.0, 6.0, (), jnp.float32)
    ancestors = draw_ancestors(jax.random.fold_in(seeds[5], 71), 0)
    return {"ancestor_inverse": ancestor_inverse, "factor": factor, "coupling": coupling, "diagonal_inverse": diagonal_inverse, "ancestors": ancestors}


def memberships(ancestors):
    block_ids = jnp.arange(NBLK, dtype=jnp.int32)
    return jnp.any(ancestors[:, :, None] == block_ids[None, None, :], axis=1)


def matmul(left, right):
    return jnp.dot(left, right, precision=lax.Precision.HIGHEST)


def reference(ancestor_inverse, factor, coupling, diagonal_inverse, ancestors):
    member = memberships(ancestors)
    row_mask = jnp.repeat(member, SN, axis=1).astype(jnp.float32)
    columns = []
    solved = {}
    for current in range(NODES):
        lower_part = factor[current].astype(jnp.float32) * row_mask[current][:, None]
        product_sum = matmul(ancestor_inverse, lower_part)
        for earlier in range(current):
            product_sum = product_sum + matmul(columns[earlier], coupling[current * (current - 1) // 2 + earlier])
        column = -product_sum
        for earlier in range(current):
            block_value = -matmul(columns[earlier].T, lower_part)
            for inner in range(current):
                block_value = block_value - matmul(solved[(earlier, inner)], coupling[current * (current - 1) // 2 + inner])
            solved[(earlier, current)] = block_value
            solved[(current, earlier)] = block_value.T
        diag_value = diagonal_inverse[current] - matmul(lower_part.T, column)
        for earlier in range(current):
            diag_value = diag_value - matmul(coupling[current * (current - 1) // 2 + earlier].T, solved[(earlier, current)])
        solved[(current, current)] = diag_value
        columns.append(column)
    block_columns = jnp.stack(columns)
    node_blocks = jnp.stack([jnp.stack([solved[(first_node, second_node)] for second_node in range(NODES)]) for first_node in range(NODES)])
    return block_columns, block_columns, node_blocks
```

```python
import jax
import jax.numpy as jnp
from jax import lax
from jax.experimental import pallas as pl
from jax.experimental.pallas import tpu as pltpu
from jax.sharding import PartitionSpec as P

MESH = pl.DeviceIdType.MESH
F32 = jnp.float32
BF16 = jnp.bfloat16
NODES = 3
SN = 512
HALF = 256
PIECE = 96
ROWS = 1536
COLS = 768
PAIRS = ((0, 0), (0, 1), (1, 1), (0, 2), (1, 2), (2, 2))


def pair_index(later, earlier):
    return later * (later - 1) // 2 + earlier


def split(value):
    high = value.astype(BF16)
    return high, (value - high.astype(F32)).astype(BF16)


def dot(left, right):
    return jnp.dot(left, right, preferred_element_type=F32)


def dot3(left, right_high, right_low):
    high, low = split(left)
    return dot(high, right_high) + dot(high, right_low) + dot(low, right_high)


def kernel(
    inverse, factor, coupling, diagonal, ancestors,
    rows_out, columns_out, upper_out,
    inv, inv_high, inv_low, own_masked, lower, partial, traded, arrived,
    couple, couple_high, couple_low, diag, tail, side, side_high, side_low,
    own_lower, tilde, tilde_other, tilde_high, tilde_low, rows_other,
    inner, recv1, recv2, recv3, part1, part2,
    local_sem, gather_send, gather_recv, lower_sem, columns_sem, trade_sem, sum_send, sum_recv,
    tilde_sem, other_sem, down_send, down_recv, up_send, up_recv, swap_sem,
):
    row = lax.axis_index("row")
    col = lax.axis_index("col")
    y, core, z, x = row // 2, row % 2, col // 4, col % 4

    def device(dy=0, dcore=0, dz=0, dx=0):
        return (
            ((y + dy) % 4) * 2 + (core + dcore) % 2,
            ((z + dz) % 4) * 4 + (x + dx) % 4,
        )

    def along(axis, step):
        return device(**{"d" + axis: step % 4})

    coordinate = {"x": x, "y": y, "z": z}
    partner = device(dcore=1)
    forward = (col // 2, (col % 2) * 8 + row)
    backward = (col % 8, 2 * row + col // 8)
    moves = jnp.logical_or(forward[0] != row, forward[1] != col)

    sent = []

    def remote(src, dst, send_sem, recv_sem, target):
        return pltpu.make_async_remote_copy(
            src_ref=src, dst_ref=dst, send_sem=send_sem, recv_sem=recv_sem,
            device_id=target, device_id_type=MESH,
        )

    def start(src, dst, send_sem, recv_sem, target):
        copy = remote(src, dst, send_sem, recv_sem, target)
        copy.start()
        sent.append(copy)
        return copy

    barrier = pltpu.get_barrier_semaphore()
    neighbours = [along(a, s) for a in "xyz" for s in (1, 2, 3)] + [partner]
    for target in neighbours:
        pl.semaphore_signal(barrier, inc=1, device_id=target, device_id_type=MESH)

    @pl.when(moves)
    def _():
        for target in (forward, backward):
            pl.semaphore_signal(barrier, inc=1, device_id=target, device_id_type=MESH)

    load_inv = pltpu.make_async_copy(inverse, inv, local_sem.at[0])
    load_couple = pltpu.make_async_copy(coupling, couple, local_sem.at[1])
    load_diag = pltpu.make_async_copy(diagonal, diag, local_sem.at[2])
    load_inv.start()
    load_couple.start()
    load_diag.start()

    first_row = (row * 16 + col) * PIECE
    first_block = first_row // SN
    last_block = (first_row + PIECE - 1) // SN
    row_at = first_row + lax.broadcasted_iota(jnp.int32, (PIECE, SN), 0)
    in_first = row_at < (first_block + 1) * SN
    for node in range(NODES):
        first_listed = jnp.float32(0)
        last_listed = jnp.float32(0)
        for slot in range(24):
            entry = ancestors[node, slot]
            first_listed = jnp.where(entry == first_block, 1.0, first_listed)
            last_listed = jnp.where(entry == last_block, 1.0, last_listed)
        keep = jnp.where(in_first, first_listed, last_listed)
        masked = jnp.where(keep > 0.5, factor[node].astype(F32), 0.0).astype(BF16)
        own_masked[node] = masked
        lower[node, 0, z, x] = masked[:, :HALF]
        lower[node, 1, z, x] = masked[:, HALF:]

    pl.semaphore_wait(barrier, len(neighbours) + 2 * jnp.where(moves, 1, 0))

    def piece(node, half, first, second):
        return lower.at[node, half, second, first] if half == 0 else lower.at[node, half, first, second]

    def line(node, half, second):
        return lower.at[node, half, second] if half == 0 else lower.at[node, half, :, second]

    def line_part(node, half, second, part):
        where = pl.ds(2 * part, 2)
        return lower.at[node, half, second, where] if half == 0 else lower.at[node, half, where, second]

    axes = ("xz", "zx")

    def gather_copy(node, half, index, ref, axis, step):
        return start(
            ref, ref, gather_send.at[node, half, index], gather_recv.at[node, half, index], along(axis, step)
        )

    copies = {}

    def first_phase(node):
        for half in range(2):
            a = axes[half][0]
            own = piece(node, half, coordinate[a], coordinate[axes[half][1]])
            copies[node, half, 0] = gather_copy(node, half, 0, own, a, 1)
            copies[node, half, 1] = gather_copy(node, half, 1, own, a, 3)

    def first_forward(node):
        for half in range(2):
            a, b = axes[half]
            for index, shift, step, cut in ((0, 3, 1, 0), (1, 1, 3, 128)):
                copies[node, half, index].wait_recv()
                got = piece(node, half, (coordinate[a] + shift) % 4, coordinate[b])
                copies[node, half, index + 2] = gather_copy(
                    node, half, index + 2, got.at[:, pl.ds(cut, 128)], a, step
                )

    def second_phase(node):
        for half in range(2):
            b = axes[half][1]
            copies[node, half, 2].wait_recv()
            copies[node, half, 3].wait_recv()
            own = line(node, half, coordinate[b])
            copies[node, half, 4] = gather_copy(node, half, 4, own, b, 1)
            copies[node, half, 5] = gather_copy(node, half, 5, own, b, 3)

    def second_forward(node):
        for half in range(2):
            b = axes[half][1]
            for index, shift, step, part in ((4, 3, 1, 0), (5, 1, 3, 1)):
                copies[node, half, index].wait_recv()
                got = line_part(node, half, (coordinate[b] + shift) % 4, part)
                copies[node, half, index + 2] = gather_copy(node, half, index + 2, got, b, step)

    def gathered(node, half):
        copies[node, half, 6].wait_recv()
        copies[node, half, 7].wait_recv()

    def multiply(node):
        for half in range(2):
            gathered(node, half)
            right = lower[node, half].reshape(ROWS, HALF)
            for part in range(4):
                rows = pl.ds(part * 192, 192)
                product = dot(inv_high[rows, :], right) + dot(inv_low[rows, :], right)
                partial[node, part, :, :, half * HALF : (half + 1) * HALF] = product.reshape(2, PIECE, HALF)
        copies["trade", node] = start(
            partial.at[node, :, 1 - core], traded.at[node], trade_sem.at[node, 0], trade_sem.at[node, 1], partner
        )

    def reduce_start(node):
        copies["trade", node].wait_recv()
        traded[node] = traded[node] + partial[node, :, core]
        for step in (1, 2, 3):
            copies["sum", node, step] = start(
                traded.at[node, (y + step) % 4], arrived.at[node, step - 1],
                sum_send.at[node, step - 1], sum_recv.at[node, step - 1], along("y", step),
            )

    def permute_copy(node, src, dst, sems, target):
        return remote(src.at[node], dst.at[node], sems.at[node, 0], sems.at[node, 1], target)

    def permute_start(node, src, dst, sems, target):
        @pl.when(moves)
        def _():
            permute_copy(node, src, dst, sems, target).start()

        @pl.when(jnp.logical_not(moves))
        def _():
            dst[node] = src[node]

    def permute_wait(node, src, dst, sems, target):
        @pl.when(moves)
        def _():
            permute_copy(node, src, dst, sems, target).wait()

    def solve(node):
        total = traded[node, y]
        for step in (1, 2, 3):
            copies["sum", node, step].wait_recv()
            total = total + arrived[node, step - 1]
        for earlier in range(node):
            g = pair_index(node, earlier)
            total = total + dot3(rows_out[earlier], couple_high[g], couple_low[g])
        rows_out[node] = -total
        permute_start(node, rows_out, columns_out, columns_sem, forward)
        copies["other", node] = start(
            rows_out.at[node], rows_other.at[node], other_sem.at[node, 0], other_sem.at[node, 1], partner
        )

    def prepare_tilde():
        for node in range(NODES):
            permute_wait(node, own_masked, own_lower, lower_sem, backward)
        for node in range(NODES):
            value = own_lower[node].astype(F32)
            for earlier in range(node):
                g = pair_index(node, earlier)
                value = value - dot3(tilde[earlier], couple_high[g], couple_low[g])
            tilde[node] = value
        copies["tilde"] = start(
            tilde.at[:, :, pl.ds(pl.multiple_of((1 - core) * HALF, HALF), HALF)], tilde_other,
            tilde_sem.at[0], tilde_sem.at[1], partner,
        )

    def transpose_tilde():
        copies["tilde"].wait_recv()
        mine = pl.ds(pl.multiple_of(core * HALF, HALF), HALF)
        for node in range(NODES):
            both = jnp.concatenate([tilde[node, :, mine], tilde_other[node]], axis=0)
            high, low = split(both.T)
            tilde_high[node] = high
            tilde_low[node] = low

    def inner_products(pairs):
        for index in pairs:
            earlier, later = PAIRS[index]
            both = jnp.concatenate([rows_out[later], rows_other[later]], axis=0)
            high, low = split(both)
            value = (
                dot(tilde_high[earlier], high) + dot(tilde_high[earlier], low) + dot(tilde_low[earlier], high)
            )
            inner[index // 2, pl.ds(index % 2 * HALF, HALF), :] = -value

    orders = ("xyz", "yzx", "zxy")
    extents = (128, 32, 8)

    def down_start(part, level, source):
        axis = orders[part][level]
        rows = extents[level]
        land = (recv1, recv2, recv3)[level]
        for step in (1, 2, 3):
            at = pl.multiple_of((coordinate[axis] + step) % 4 * rows, rows)
            copies["down", part, level, step] = start(
                source.at[pl.ds(at, rows)], land.at[part, step - 1],
                down_send.at[part, level, step - 1], down_recv.at[part, level, step - 1], along(axis, step),
            )

    def down_finish(part, level, source):
        axis = orders[part][level]
        rows = extents[level]
        land = (recv1, recv2, recv3)[level]
        total = source[pl.ds(pl.multiple_of(coordinate[axis] * rows, rows), rows), :]
        for step in (1, 2, 3):
            copies["down", part, level, step].wait_recv()
            total = total + land[part, step - 1]
        return total

    def offset(part, levels):
        at = 0
        for level in range(levels):
            at = at + coordinate[orders[part][level]] * extents[level]
        return at

    def up_start(part, level):
        axis = orders[part][level]
        rows = extents[level]
        at = pl.multiple_of(offset(part, level + 1), rows)
        ref = upper_out.at[core, part, pl.ds(at, rows)]
        for step in (1, 2, 3):
            copies["up", part, level, step] = start(
                ref, ref, up_send.at[part, level, step - 1], up_recv.at[part, level, step - 1], along(axis, step)
            )

    def up_wait(part, level):
        for step in (1, 2, 3):
            copies["up", part, level, step].wait_recv()

    def swap(part):
        ref = upper_out.at[core, part]
        copies["swap", part] = start(ref, ref, swap_sem.at[part, 0], swap_sem.at[part, 1], partner)

    def split_side(value):
        high, low = split(value)
        side_high[...] = high
        side_low[...] = low

    def add_product(target, left, high, low, base):
        def body(block, carry):
            rows = pl.ds(pl.multiple_of(block * 128, 128), 128)
            target[rows, :] = base[rows, :] - dot3(left[rows, :], high[...], low[...])
            return carry

        lax.fori_loop(0, 4, body, 0)

    def negate_product(target, left, high, low):
        def body(block, carry):
            rows = pl.ds(pl.multiple_of(block * 128, 128), 128)
            target[rows, :] = -dot3(left[rows, :], high[...], low[...])
            return carry

        lax.fori_loop(0, 4, body, 0)

    e00, e01, e11, e02, e12, e22 = (tail.at[i] for i in range(6))

    def tail_first():
        e00[...] = diag[0]
        negate_product(e01, diag.at[0], couple_high.at[0], couple_low.at[0])
        negate_product(e02, diag.at[0], couple_high.at[1], couple_low.at[1])
        add_product(e02, e01, couple_high.at[2], couple_low.at[2], e02)

    def tail_second():
        split_side(e01[...])
        side[...] = couple[0].T
        add_product(e11, side, side_high, side_low, diag.at[1])
        side[...] = e01[...].T
        negate_product(e12, side, couple_high.at[1], couple_low.at[1])
        add_product(e12, e11, couple_high.at[2], couple_low.at[2], e12)

    def tail_third():
        split_side(e02[...])
        side[...] = couple[1].T
        add_product(e22, side, side_high, side_low, diag.at[2])
        split_side(e12[...])
        side[...] = couple[2].T
        add_product(e22, side, side_high, side_low, e22)

    for node in range(NODES):
        first_phase(node)
        permute_start(node, own_masked, own_lower, lower_sem, backward)
    load_inv.wait()
    first_forward(0)
    second_phase(0)
    first_forward(1)
    first_forward(2)
    for block in range(6):
        where = slice(block * 256, (block + 1) * 256)
        high, low = split(inv[where, :].T)
        inv_high[:, where] = high
        inv_low[:, where] = low
    second_forward(0)
    second_phase(1)
    load_couple.wait()
    load_diag.wait()
    for g in range(3):
        high, low = split(couple[g])
        couple_high[g] = high
        couple_low[g] = low
    multiply(0)
    second_forward(1)
    second_phase(2)
    reduce_start(0)
    tail_first()
    multiply(1)
    second_forward(2)
    reduce_start(1)
    prepare_tilde()
    tail_second()
    solve(0)
    multiply(2)
    reduce_start(2)
    transpose_tilde()
    solve(1)
    tail_third()
    copies["other", 0].wait_recv()
    copies["other", 1].wait_recv()
    inner_products((0, 1, 2))
    down_start(0, 0, inner.at[0])
    solve(2)
    copies["other", 2].wait_recv()
    inner_products((3,))
    down_start(1, 0, inner.at[1])
    inner_products((4, 5))
    down_start(2, 0, inner.at[2])
    for part in range(3):
        part1[part] = down_finish(part, 0, inner.at[part])
        down_start(part, 1, part1.at[part])
    for part in range(3):
        part2[part] = down_finish(part, 1, part1.at[part])
        down_start(part, 2, part2.at[part])
    for part in range(3):
        at = offset(part, 3)
        base = tail[2 * part + at // HALF, pl.ds(pl.multiple_of(core * HALF + at % HALF, 8), 8), :]
        upper_out[core, part, pl.ds(pl.multiple_of(at, 8), 8), :] = base + down_finish(part, 2, part2.at[part])
        up_start(part, 2)
    for level in (1, 0):
        for part in range(3):
            up_wait(part, level + 1)
            up_start(part, level)
    for part in range(3):
        up_wait(part, 0)
        swap(part)
    for part in range(3):
        copies["swap", part].wait_recv()
    for node in range(NODES):
        permute_wait(node, rows_out, columns_out, columns_sem, forward)
    for copy in sent:
        copy.wait_send()


def fused(ancestor_inverse, factor, coupling, diagonal_inverse, ancestors):
    vmem = pl.BlockSpec(memory_space=pltpu.VMEM)
    hbm = pl.BlockSpec(memory_space=pl.ANY)
    dma = pltpu.SemaphoreType.DMA
    square = (SN, SN)
    return pl.pallas_call(
        kernel,
        out_shape=(
            jax.ShapeDtypeStruct((NODES, PIECE, SN), F32),
            jax.ShapeDtypeStruct((NODES, PIECE, SN), F32),
            jax.ShapeDtypeStruct((2, 3, SN, SN), F32),
        ),
        in_specs=[hbm, vmem, hbm, hbm, pl.BlockSpec(memory_space=pltpu.SMEM)],
        out_specs=(vmem, vmem, vmem),
        scratch_shapes=[
            pltpu.VMEM((ROWS, COLS), F32),
            pltpu.VMEM((COLS, ROWS), BF16),
            pltpu.VMEM((COLS, ROWS), BF16),
            pltpu.VMEM((NODES, PIECE, SN), BF16),
            pltpu.VMEM((NODES, 2, 4, 4, PIECE, HALF), BF16),
            pltpu.VMEM((NODES, 4, 2, PIECE, SN), F32),
            pltpu.VMEM((NODES, 4, PIECE, SN), F32),
            pltpu.VMEM((NODES, 3, PIECE, SN), F32),
            pltpu.VMEM((3,) + square, F32),
            pltpu.VMEM((3,) + square, BF16),
            pltpu.VMEM((3,) + square, BF16),
            pltpu.VMEM((3,) + square, F32),
            pltpu.VMEM((6,) + square, F32),
            pltpu.VMEM(square, F32),
            pltpu.VMEM(square, BF16),
            pltpu.VMEM(square, BF16),
            pltpu.VMEM((NODES, PIECE, SN), BF16),
            pltpu.VMEM((NODES, PIECE, SN), F32),
            pltpu.VMEM((NODES, PIECE, HALF), F32),
            pltpu.VMEM((NODES, HALF, 2 * PIECE), BF16),
            pltpu.VMEM((NODES, HALF, 2 * PIECE), BF16),
            pltpu.VMEM((NODES, PIECE, SN), F32),
            pltpu.VMEM((3,) + square, F32),
            pltpu.VMEM((3, 3, 128, SN), F32),
            pltpu.VMEM((3, 3, 32, SN), F32),
            pltpu.VMEM((3, 3, 8, SN), F32),
            pltpu.VMEM((3, 128, SN), F32),
            pltpu.VMEM((3, 32, SN), F32),
            dma((3,)),
            dma((NODES, 2, 8)),
            dma((NODES, 2, 8)),
            dma((NODES, 2)),
            dma((NODES, 2)),
            dma((NODES, 2)),
            dma((NODES, 3)),
            dma((NODES, 3)),
            dma((2,)),
            dma((NODES, 2)),
            dma((3, 3, 3)),
            dma((3, 3, 3)),
            dma((3, 3, 3)),
            dma((3, 3, 3)),
            dma((3, 2)),
        ],
        compiler_params=pltpu.CompilerParams(
            collective_id=0, has_side_effects=True, vmem_limit_bytes=62 << 20
        ),
        name="selected_inversion",
    )(ancestor_inverse, factor, coupling, diagonal_inverse, ancestors)


def local(ancestor_inverse, factor, coupling, diagonal_inverse, ancestors):
    block_rows, block_columns, upper = fused(
        ancestor_inverse, factor, coupling, diagonal_inverse, ancestors
    )
    blocks = {}
    for index, (earlier, later) in enumerate(PAIRS):
        part = upper[:, index // 2, index % 2 * HALF : (index % 2 + 1) * HALF]
        blocks[earlier, later] = part.reshape(SN, SN)
    for earlier, later in PAIRS:
        if earlier != later:
            blocks[later, earlier] = blocks[earlier, later].T
    node_blocks = jnp.stack([jnp.stack([blocks[j, k] for k in range(NODES)]) for j in range(NODES)])
    return block_columns, block_rows, node_blocks


def solution(mesh):
    placed = (P("row", "col"), P(None, ("row", "col"), None), P(), P(), P())
    return jax.shard_map(
        local,
        mesh=mesh,
        in_specs=placed,
        out_specs=(P(None, ("row", "col"), None), P(None, ("col", "row"), None), P()),
        check_vma=False,
    )
```

```python
import jax
import jax.numpy as jnp
from jax import lax
from jax.experimental import pallas as pl
from jax.experimental.pallas import tpu as pltpu
from jax.sharding import PartitionSpec as P

MESH = pl.DeviceIdType.MESH
F32 = jnp.float32
BF16 = jnp.bfloat16
NODES = 3
SN = 512
HALF = 256
PIECE = 96
ROWS = 1536
COLS = 768
QUARTER = 128


def pair_index(later, earlier):
    return later * (later - 1) // 2 + earlier


def split(value):
    high = value.astype(BF16)
    return high, (value - high.astype(F32)).astype(BF16)


def dot(left, right):
    return jnp.dot(left, right, preferred_element_type=F32)


def dot3(left, right_high, right_low):
    high, low = split(left)
    return dot(high, right_high) + dot(high, right_low) + dot(low, right_high)


def first_block(node):
    return node * (node + 1) // 2


def kernel(
    inverse, factor, coupling, diagonal, ancestors,
    rows_out, columns_out, blocks_out,
    inv, inv_high, inv_low, own_masked, lower, partial, traded, arrived, solved,
    couple, couple_high, couple_low, diag, tail, side, side_high, side_low,
    column_lower, tilde_high, tilde_low, inner, inner_recv, inner_sum, inner_last,
    local_sem, gather_send, gather_recv, lower_sem, spread_send, spread_recv, both_sem, columns_sem, trade_sem,
    sum_send, sum_recv, rows_send, rows_recv, swap_sem, down_send, down_recv, up_send, up_recv, pair_send, pair_recv,
):
    row = lax.axis_index("row")
    col = lax.axis_index("col")
    y, core, z, x = row // 2, row % 2, col // 4, col % 4

    def device(dy=0, dcore=0, dz=0, dx=0):
        return (
            ((y + dy) % 4) * 2 + (core + dcore) % 2,
            ((z + dz) % 4) * 4 + (x + dx) % 4,
        )

    def along(axis, step):
        return device(**{"d" + axis: step % 4})

    coordinate = {"x": x, "y": y, "z": z}
    partner = device(dcore=1)
    forward = (col // 2, (col % 2) * 8 + row)
    backward = (col % 8, 2 * row + col // 8)
    moves = jnp.logical_or(forward[0] != row, forward[1] != col)
    lower_to = (x * 2 + z % 2, y * 4 + 2 * core + z // 2)
    lower_from = (z * 2 + x // 2, (2 * (x % 2) + core) * 4 + y)
    lower_moves = jnp.logical_or(lower_to[0] != row, lower_to[1] != col)

    sent = []
    copies = {}

    def remote(src, dst, send_sem, recv_sem, target):
        return pltpu.make_async_remote_copy(
            src_ref=src, dst_ref=dst, send_sem=send_sem, recv_sem=recv_sem,
            device_id=target, device_id_type=MESH,
        )

    def start(src, dst, send_sem, recv_sem, target):
        copy = remote(src, dst, send_sem, recv_sem, target)
        copy.start()
        sent.append(copy)
        return copy

    barrier = pltpu.get_barrier_semaphore()
    neighbours = [along(a, s) for a in "xyz" for s in (1, 2, 3)] + [partner]
    for target in neighbours:
        pl.semaphore_signal(barrier, inc=1, device_id=target, device_id_type=MESH)

    @pl.when(moves)
    def _():
        for target in (forward, backward):
            pl.semaphore_signal(barrier, inc=1, device_id=target, device_id_type=MESH)

    @pl.when(lower_moves)
    def _():
        for target in (lower_to, lower_from):
            pl.semaphore_signal(barrier, inc=1, device_id=target, device_id_type=MESH)

    load_inv = pltpu.make_async_copy(inverse, inv, local_sem.at[0])
    load_couple = pltpu.make_async_copy(coupling, couple, local_sem.at[1])
    load_diag = pltpu.make_async_copy(diagonal, diag, local_sem.at[2])
    load_inv.start()
    load_couple.start()
    load_diag.start()

    first_row = (row * 16 + col) * PIECE
    block_first = first_row // SN
    block_last = (first_row + PIECE - 1) // SN
    row_at = first_row + lax.broadcasted_iota(jnp.int32, (PIECE, SN), 0)
    in_first = row_at < (block_first + 1) * SN
    for node in range(NODES):
        first_listed = jnp.float32(0)
        last_listed = jnp.float32(0)
        for slot in range(24):
            entry = ancestors[node, slot]
            first_listed = jnp.where(entry == block_first, 1.0, first_listed)
            last_listed = jnp.where(entry == block_last, 1.0, last_listed)
        keep = jnp.where(in_first, first_listed, last_listed)
        masked = jnp.where(keep > 0.5, factor[node].astype(F32), 0.0).astype(BF16)
        own_masked[node] = masked
        lower[node, 0, z, x] = masked[:, :HALF]
        lower[node, 1, z, x] = masked[:, HALF:]

    pl.semaphore_wait(
        barrier, len(neighbours) + 2 * jnp.where(moves, 1, 0) + 2 * jnp.where(lower_moves, 1, 0)
    )

    def piece(node, half, first, second):
        return lower.at[node, half, second, first] if half == 0 else lower.at[node, half, first, second]

    def line(node, half, second):
        return lower.at[node, half, second] if half == 0 else lower.at[node, half, :, second]

    def line_part(node, half, second, part):
        where = pl.ds(2 * part, 2)
        return lower.at[node, half, second, where] if half == 0 else lower.at[node, half, where, second]

    axes = ("xz", "zx")

    def gather_copy(node, half, index, ref, axis, step):
        return start(
            ref, ref, gather_send.at[node, half, index], gather_recv.at[node, half, index], along(axis, step)
        )

    def first_phase(node):
        for half in range(2):
            a = axes[half][0]
            own = piece(node, half, coordinate[a], coordinate[axes[half][1]])
            copies[node, half, 0] = gather_copy(node, half, 0, own, a, 1)
            copies[node, half, 1] = gather_copy(node, half, 1, own, a, 3)

    def first_forward(node):
        for half in range(2):
            a, b = axes[half]
            for index, shift, step, cut in ((0, 3, 1, 0), (1, 1, 3, 128)):
                copies[node, half, index].wait_recv()
                got = piece(node, half, (coordinate[a] + shift) % 4, coordinate[b])
                copies[node, half, index + 2] = gather_copy(
                    node, half, index + 2, got.at[:, pl.ds(cut, 128)], a, step
                )

    def second_phase(node):
        for half in range(2):
            b = axes[half][1]
            copies[node, half, 2].wait_recv()
            copies[node, half, 3].wait_recv()
            own = line(node, half, coordinate[b])
            copies[node, half, 4] = gather_copy(node, half, 4, own, b, 1)
            copies[node, half, 5] = gather_copy(node, half, 5, own, b, 3)

    def second_forward(node):
        for half in range(2):
            b = axes[half][1]
            for index, shift, step, part in ((4, 3, 1, 0), (5, 1, 3, 1)):
                copies[node, half, index].wait_recv()
                got = line_part(node, half, (coordinate[b] + shift) % 4, part)
                copies[node, half, index + 2] = gather_copy(node, half, index + 2, got, b, step)

    def gathered(node, half):
        copies[node, half, 6].wait_recv()
        copies[node, half, 7].wait_recv()

    def multiply(node):
        for half in range(2):
            gathered(node, half)
            right = lower[node, half].reshape(ROWS, HALF)
            for part in range(4):
                rows = pl.ds(part * 192, 192)
                product = dot(inv_high[rows, :], right) + dot(inv_low[rows, :], right)
                partial[node, part, :, :, half * HALF : (half + 1) * HALF] = product.reshape(2, PIECE, HALF)
        copies["trade", node] = start(
            partial.at[node, :, 1 - core], traded.at[node], trade_sem.at[node, 0], trade_sem.at[node, 1], partner
        )

    def chain(later, earlier):
        g = pair_index(later, earlier)

        def body(part, carry):
            partial[later, part, core] = partial[later, part, core] + dot3(
                traded[earlier, part], couple_high[g], couple_low[g]
            )
            return carry

        lax.fori_loop(0, 4, body, 0)

    def reduce_start(node):
        copies["trade", node].wait_recv()
        traded[node] = -(traded[node] + partial[node, :, core])
        for step in (1, 2, 3):
            at = pl.multiple_of((y + step) % 4 * QUARTER, QUARTER)
            copies["sum", node, step] = start(
                traded.at[node, :, :, pl.ds(at, QUARTER)], arrived.at[node, step - 1],
                sum_send.at[node, step - 1], sum_recv.at[node, step - 1], along("y", step),
            )

    def finish(node):
        at = pl.multiple_of(y * QUARTER, QUARTER)
        total = traded[node, :, :, pl.ds(at, QUARTER)]
        for step in (1, 2, 3):
            copies["sum", node, step].wait_recv()
            total = total + arrived[node, step - 1]
        solved[node, :, core] = total
        ref = solved.at[node, :, core]
        copies["swap", node] = start(ref, ref, swap_sem.at[node, 0], swap_sem.at[node, 1], partner)

    def rows_start(node):
        at = pl.multiple_of(y * QUARTER, QUARTER)
        where = (node, slice(None), pl.ds(at, QUARTER))
        for step in (1, 2, 3):
            copies["rows", node, step] = start(
                solved.at[node, (y + step) % 4, core], rows_out.at[where],
                rows_send.at[node, step - 1], rows_recv.at[node, step - 1], along("y", step),
            )
        rows_out[where] = solved[node, y, core]

    def columns_copy(node):
        return remote(
            rows_out.at[node], columns_out.at[node], columns_sem.at[node, 0], columns_sem.at[node, 1], forward
        )

    def columns_start(node):
        for step in (1, 2, 3):
            copies["rows", node, step].wait_recv()

        @pl.when(moves)
        def _():
            columns_copy(node).start()

        @pl.when(jnp.logical_not(moves))
        def _():
            columns_out[node] = rows_out[node]

    def columns_wait(node):
        @pl.when(moves)
        def _():
            columns_copy(node).wait()

    def lower_copy():
        return remote(
            own_masked, column_lower.at[:, z % 2, x], lower_sem.at[0], lower_sem.at[1], lower_to
        )

    def lower_start():
        @pl.when(lower_moves)
        def _():
            lower_copy().start()

        @pl.when(jnp.logical_not(lower_moves))
        def _():
            for node in range(NODES):
                column_lower[node, core, y] = own_masked[node]

    def lower_spread():
        @pl.when(lower_moves)
        def _():
            lower_copy().wait()

        ref = column_lower.at[:, core, y]
        for step in (1, 2, 3):
            copies["spread", step] = start(
                ref, ref, spread_send.at[step - 1], spread_recv.at[step - 1], along("y", step)
            )

    def lower_both():
        for step in (1, 2, 3):
            copies["spread", step].wait_recv()
        ref = column_lower.at[:, core]
        copies["both"] = start(ref, ref, both_sem.at[0], both_sem.at[1], partner)

    def prepare_tilde():
        copies["both"].wait_recv()
        for side_core in range(2):
            for part in range(4):
                rows = pl.ds((side_core * 4 + part) * PIECE, PIECE)
                for node in range(NODES):
                    own = column_lower[node, side_core, part]
                    if node == 0:
                        tilde_high[0, rows, :] = own
                        continue
                    first = column_lower[0, side_core, part]
                    g = pair_index(node, 0)
                    value = own.astype(F32) - (dot(first, couple_high[g]) + dot(first, couple_low[g]))
                    if node == 2:
                        high, low = tilde_high[1, rows, :], tilde_low[1, rows, :]
                        g = pair_index(2, 1)
                        value = value - (
                            dot(high, couple_high[g]) + dot(high, couple_low[g]) + dot(low, couple_high[g])
                        )
                    high, low = split(value)
                    tilde_high[node, rows, :] = high
                    tilde_low[node, rows, :] = low

    def inner_products(later):
        copies["swap", later].wait_recv()
        high, low = split(solved[later].reshape(COLS, QUARTER).T)
        mine = pl.ds(pl.multiple_of(core * HALF, HALF), HALF)
        for earlier in range(later + 1):
            right = tilde_high[earlier, :, mine]
            value = dot(high, right) + dot(low, right)
            if earlier > 0:
                value = value + dot(high, tilde_low[earlier, :, mine])
            for half in range(2):
                cut = value[:, half * QUARTER : (half + 1) * QUARTER]
                inner[half, first_block(later) + earlier] = -cut.reshape(4, 4, 8, QUARTER)

    def down_start(node, level):
        group = slice(first_block(node), first_block(node) + node + 1)
        for half in range(2):
            axis = ("xz", "zx")[half][level]
            for step in (1, 2, 3):
                target = (coordinate[axis] + step) % 4
                if level == 1:
                    src, dst = inner_sum.at[half, group, target], inner_last.at[half, step - 1, group]
                else:
                    src = inner.at[0, group, target] if half == 0 else inner.at[1, group, :, target]
                    dst = inner_recv.at[half, step - 1, group]
                sems = (node, level, half, step - 1)
                copies["down", node, level, half, step] = start(
                    src, dst, down_send.at[sems], down_recv.at[sems], along(axis, step)
                )

    def down_finish(node, level, half):
        group = slice(first_block(node), first_block(node) + node + 1)
        axis = ("xz", "zx")[half][level]
        own = coordinate[axis]
        if level == 1:
            total = inner_sum[half, group, own]
        else:
            total = inner[0, group, own] if half == 0 else inner[1, group, :, own]
        land = (inner_recv, inner_last)[level]
        for step in (1, 2, 3):
            copies["down", node, level, half, step].wait_recv()
            total = total + land[half, step - 1, group]
        return total

    def down_middle(node):
        group = slice(first_block(node), first_block(node) + node + 1)
        for half in range(2):
            inner_sum[half, group] = down_finish(node, 0, half)
        down_start(node, 1)

    def down_last(node):
        rows = pl.ds(pl.multiple_of(y * 128 + x * 32 + z * 8, 8), 8)
        for half in range(2):
            total = down_finish(node, 1, half)
            lanes = pl.ds(pl.multiple_of(core * HALF + half * QUARTER, QUARTER), QUARTER)
            for earlier in range(node + 1):
                block = first_block(node) + earlier
                blocks_out[block, core, half, y, x, z] = tail[block, rows, lanes] + total[earlier]

    orders = ("zxy", "yzx", "xyz")

    def up_ref(block, level, **other):
        done = orders[block % 3][:level]
        where = [other.get(a, slice(None) if a in done else coordinate[a]) for a in "yxz"]
        return blocks_out.at[(block, core, slice(None), *where)]

    def up_start(block, level):
        axis = orders[block % 3][level]
        ref = up_ref(block, level)
        for step in (1, 2, 3):
            sems = (block, level, step - 1)
            copies["up", block, level, step] = start(ref, ref, up_send.at[sems], up_recv.at[sems], along(axis, step))

    def up_wait(block, level):
        for step in (1, 2, 3):
            copies["up", block, level, step].wait_recv()

    def pair_start(block, step):
        axis = orders[block % 3][2]
        ref = up_ref(block, 2, **{axis: (coordinate[axis] - step) % 4})
        copies["pair", block, step] = start(ref, ref, pair_send.at[block, step], pair_recv.at[block, step], partner)

    def up_all(group):
        for level in range(3):
            for block in group:
                if level > 0:
                    up_wait(block, level - 1)
                up_start(block, level)
                if level == 2:
                    pair_start(block, 0)

    def pair_rest(group):
        for step in (1, 3, 2):
            for block in group:
                copies["up", block, 2, step].wait_recv()
                pair_start(block, step)

    def split_side(value):
        high, low = split(value)
        side_high[...] = high
        side_low[...] = low

    def add_product(target, left, high, low, base):
        def body(block, carry):
            rows = pl.ds(pl.multiple_of(block * 128, 128), 128)
            target[rows, :] = base[rows, :] - dot3(left[rows, :], high[...], low[...])
            return carry

        lax.fori_loop(0, 4, body, 0)

    def negate_product(target, left, high, low):
        def body(block, carry):
            rows = pl.ds(pl.multiple_of(block * 128, 128), 128)
            target[rows, :] = -dot3(left[rows, :], high[...], low[...])
            return carry

        lax.fori_loop(0, 4, body, 0)

    e00, e01, e11, e02, e12, e22 = (tail.at[i] for i in (0, 1, 2, 3, 4, 5))

    def tail_first():
        e00[...] = diag[0]
        negate_product(e01, diag.at[0], couple_high.at[0], couple_low.at[0])
        negate_product(e02, diag.at[0], couple_high.at[1], couple_low.at[1])
        add_product(e02, e01, couple_high.at[2], couple_low.at[2], e02)

    def tail_second():
        split_side(e01[...])
        side[...] = couple[0].T
        add_product(e11, side, side_high, side_low, diag.at[1])
        e01[...] = e01[...].T
        negate_product(e12, e01, couple_high.at[1], couple_low.at[1])
        add_product(e12, e11, couple_high.at[2], couple_low.at[2], e12)

    def tail_third():
        split_side(e02[...])
        side[...] = couple[1].T
        add_product(e22, side, side_high, side_low, diag.at[2])
        split_side(e12[...])
        side[...] = couple[2].T
        add_product(e22, side, side_high, side_low, e22)
        e02[...] = e02[...].T
        e12[...] = e12[...].T

    for node in range(NODES):
        first_phase(node)
    load_inv.wait()
    first_forward(0)
    second_phase(0)
    first_forward(1)
    first_forward(2)
    lower_start()
    for block in range(6):
        where = slice(block * 256, (block + 1) * 256)
        high, low = split(inv[where, :].T)
        inv_high[:, where] = high
        inv_low[:, where] = low
    second_forward(0)
    second_phase(1)
    load_couple.wait()
    load_diag.wait()
    for g in range(3):
        high, low = split(couple[g])
        couple_high[g] = high
        couple_low[g] = low
    multiply(0)
    second_forward(1)
    second_phase(2)
    lower_spread()
    reduce_start(0)
    tail_first()
    multiply(1)
    chain(1, 0)
    second_forward(2)
    lower_both()
    reduce_start(1)
    finish(0)
    rows_start(0)
    tail_second()
    multiply(2)
    chain(2, 0)
    chain(2, 1)
    reduce_start(2)
    columns_start(0)
    prepare_tilde()
    inner_products(0)
    down_start(0, 0)
    finish(1)
    rows_start(1)
    inner_products(1)
    down_start(1, 0)
    tail_third()
    down_middle(0)
    down_middle(1)
    columns_start(1)
    down_last(0)
    down_last(1)
    up_all((0, 1, 2))
    finish(2)
    rows_start(2)
    inner_products(2)
    down_start(2, 0)
    pair_rest((0, 1, 2))
    down_middle(2)
    columns_start(2)
    down_last(2)
    up_all((3, 4, 5))
    pair_rest((3, 4, 5))
    for block in range(6):
        for step in range(4):
            copies["pair", block, step].wait_recv()
    for node in range(NODES):
        columns_wait(node)
    for copy in sent:
        copy.wait_send()


def fused(ancestor_inverse, factor, coupling, diagonal_inverse, ancestors):
    vmem = pl.BlockSpec(memory_space=pltpu.VMEM)
    hbm = pl.BlockSpec(memory_space=pl.ANY)
    dma = pltpu.SemaphoreType.DMA
    square = (SN, SN)
    return pl.pallas_call(
        kernel,
        out_shape=(
            jax.ShapeDtypeStruct((NODES, PIECE, SN), F32),
            jax.ShapeDtypeStruct((NODES, PIECE, SN), F32),
            jax.ShapeDtypeStruct((6, 2, 2, 4, 4, 4, 8, QUARTER), F32),
        ),
        in_specs=[hbm, vmem, hbm, hbm, pl.BlockSpec(memory_space=pltpu.SMEM)],
        out_specs=(vmem, vmem, vmem),
        scratch_shapes=[
            pltpu.VMEM((ROWS, COLS), F32),
            pltpu.VMEM((COLS, ROWS), BF16),
            pltpu.VMEM((COLS, ROWS), BF16),
            pltpu.VMEM((NODES, PIECE, SN), BF16),
            pltpu.VMEM((NODES, 2, 4, 4, PIECE, HALF), BF16),
            pltpu.VMEM((NODES, 4, 2, PIECE, SN), F32),
            pltpu.VMEM((NODES, 4, PIECE, SN), F32),
            pltpu.VMEM((NODES, 3, 4, PIECE, QUARTER), F32),
            pltpu.VMEM((NODES, 4, 2, PIECE, QUARTER), F32),
            pltpu.VMEM((3,) + square, F32),
            pltpu.VMEM((3,) + square, BF16),
            pltpu.VMEM((3,) + square, BF16),
            pltpu.VMEM((3,) + square, F32),
            pltpu.VMEM((6,) + square, F32),
            pltpu.VMEM(square, F32),
            pltpu.VMEM(square, BF16),
            pltpu.VMEM(square, BF16),
            pltpu.VMEM((NODES, 2, 4, PIECE, SN), BF16),
            pltpu.VMEM((NODES, COLS, SN), BF16),
            pltpu.VMEM((NODES, COLS, SN), BF16),
            pltpu.VMEM((2, 6, 4, 4, 8, QUARTER), F32),
            pltpu.VMEM((2, 3, 6, 4, 8, QUARTER), F32),
            pltpu.VMEM((2, 6, 4, 8, QUARTER), F32),
            pltpu.VMEM((2, 3, 6, 8, QUARTER), F32),
            dma((3,)),
            dma((NODES, 2, 8)),
            dma((NODES, 2, 8)),
            dma((2,)),
            dma((3,)),
            dma((3,)),
            dma((2,)),
            dma((NODES, 2)),
            dma((NODES, 2)),
            dma((NODES, 3)),
            dma((NODES, 3)),
            dma((NODES, 3)),
            dma((NODES, 3)),
            dma((NODES, 2)),
            dma((NODES, 2, 2, 3)),
            dma((NODES, 2, 2, 3)),
            dma((6, 3, 3)),
            dma((6, 3, 3)),
            dma((6, 4)),
            dma((6, 4)),
        ],
        compiler_params=pltpu.CompilerParams(
            collective_id=0, has_side_effects=True, vmem_limit_bytes=63 << 20
        ),
        name="selected_inversion",
    )(ancestor_inverse, factor, coupling, diagonal_inverse, ancestors)


def assemble_kernel(block, out):
    def lanes(half):
        return block[0, half // 2, half % 2].reshape(SN, QUARTER)

    upper = pl.program_id(0) < pl.program_id(1)

    @pl.when(jnp.logical_not(upper))
    def _():
        for half in range(4):
            out[0, 0, :, half * QUARTER : (half + 1) * QUARTER] = lanes(half)

    @pl.when(upper)
    def _():
        for half in range(4):
            out[0, 0, half * QUARTER : (half + 1) * QUARTER, :] = lanes(half).T


def assemble(blocks):
    def at(first, second):
        later, earlier = jnp.maximum(first, second), jnp.minimum(first, second)
        return (later * (later + 1) // 2 + earlier,) + (0,) * 7

    return pl.pallas_call(
        assemble_kernel,
        out_shape=jax.ShapeDtypeStruct((NODES, NODES, SN, SN), F32),
        grid=(NODES, NODES),
        in_specs=[pl.BlockSpec((1, 2, 2, 4, 4, 4, 8, QUARTER), at)],
        out_specs=pl.BlockSpec((1, 1, SN, SN), lambda first, second: (first, second, 0, 0)),
        compiler_params=pltpu.CompilerParams(vmem_limit_bytes=16 << 20),
        name="assemble_node_blocks",
    )(blocks)


def local(ancestor_inverse, factor, coupling, diagonal_inverse, ancestors):
    block_rows, block_columns, blocks = fused(
        ancestor_inverse, factor, coupling, diagonal_inverse, ancestors
    )
    return block_columns, block_rows, assemble(blocks)


def solution(mesh):
    placed = (P("row", "col"), P(None, ("row", "col"), None), P(), P(), P())
    return jax.shard_map(
        local,
        mesh=mesh,
        in_specs=placed,
        out_specs=(P(None, ("row", "col"), None), P(None, ("col", "row"), None), P()),
        check_vma=False,
    )
```

```python
import jax
import jax.numpy as jnp
from jax import lax
from jax.experimental import pallas as pl
from jax.experimental.pallas import tpu as pltpu
from jax.sharding import PartitionSpec as P

MESH = pl.DeviceIdType.MESH
F32 = jnp.float32
BF16 = jnp.bfloat16
NODES = 3
SN = 512
HALF = 256
PIECE = 96
ROWS = 1536
COLS = 768
QUARTER = 128


def pair_index(later, earlier):
    return later * (later - 1) // 2 + earlier


def split(value):
    high = value.astype(BF16)
    return high, (value - high.astype(F32)).astype(BF16)


def dot(left, right):
    return jnp.dot(left, right, preferred_element_type=F32)


def dot3(left, right_high, right_low):
    high, low = split(left)
    return dot(high, right_high) + dot(high, right_low) + dot(low, right_high)


def first_block(node):
    return node * (node + 1) // 2


def kernel(
    inverse, factor, coupling, diagonal, ancestors,
    rows_out, columns_out, blocks_out,
    inv, inv_high, inv_low, own_masked, lower, partial, traded, correct, arrived, solved,
    couple, couple_high, couple_low, diag, tail, side, side_high, side_low,
    column_lower, tilde_high, tilde_low, inner, inner_recv, inner_sum, inner_last,
    local_sem, gather_send, gather_recv, lower_sem, spread_send, spread_recv, both_sem, columns_sem, trade_sem,
    sum_send, sum_recv, rows_send, rows_recv, swap_sem, down_send, down_recv, up_send, up_recv, pair_send, pair_recv,
):
    row = lax.axis_index("row")
    col = lax.axis_index("col")
    y, core, z, x = row // 2, row % 2, col // 4, col % 4

    def device(dy=0, dcore=0, dz=0, dx=0):
        return (
            ((y + dy) % 4) * 2 + (core + dcore) % 2,
            ((z + dz) % 4) * 4 + (x + dx) % 4,
        )

    def along(axis, step):
        return device(**{"d" + axis: step % 4})

    coordinate = {"x": x, "y": y, "z": z}
    partner = device(dcore=1)
    forward = (col // 2, (col % 2) * 8 + row)
    backward = (col % 8, 2 * row + col // 8)
    moves = jnp.logical_or(forward[0] != row, forward[1] != col)
    lower_to = (x * 2 + z % 2, y * 4 + 2 * core + z // 2)
    lower_from = (z * 2 + x // 2, (2 * (x % 2) + core) * 4 + y)
    lower_moves = jnp.logical_or(lower_to[0] != row, lower_to[1] != col)

    sent = []
    copies = {}

    def remote(src, dst, send_sem, recv_sem, target):
        return pltpu.make_async_remote_copy(
            src_ref=src, dst_ref=dst, send_sem=send_sem, recv_sem=recv_sem,
            device_id=target, device_id_type=MESH,
        )

    def start(src, dst, send_sem, recv_sem, target):
        copy = remote(src, dst, send_sem, recv_sem, target)
        copy.start()
        sent.append(copy)
        return copy

    barrier = pltpu.get_barrier_semaphore()
    neighbours = [along(a, s) for a in "xyz" for s in (1, 2, 3)] + [partner]
    for target in neighbours:
        pl.semaphore_signal(barrier, inc=1, device_id=target, device_id_type=MESH)

    @pl.when(moves)
    def _():
        for target in (forward, backward):
            pl.semaphore_signal(barrier, inc=1, device_id=target, device_id_type=MESH)

    @pl.when(lower_moves)
    def _():
        for target in (lower_to, lower_from):
            pl.semaphore_signal(barrier, inc=1, device_id=target, device_id_type=MESH)

    load_inv = pltpu.make_async_copy(inverse, inv, local_sem.at[0])
    load_couple = pltpu.make_async_copy(coupling, couple, local_sem.at[1])
    load_diag = pltpu.make_async_copy(diagonal, diag, local_sem.at[2])
    load_inv.start()
    load_couple.start()
    load_diag.start()

    first_row = (row * 16 + col) * PIECE
    block_first = first_row // SN
    block_last = (first_row + PIECE - 1) // SN
    row_at = first_row + lax.broadcasted_iota(jnp.int32, (PIECE, SN), 0)
    in_first = row_at < (block_first + 1) * SN
    for node in range(NODES):
        first_listed = jnp.float32(0)
        last_listed = jnp.float32(0)
        for slot in range(24):
            entry = ancestors[node, slot]
            first_listed = jnp.where(entry == block_first, 1.0, first_listed)
            last_listed = jnp.where(entry == block_last, 1.0, last_listed)
        keep = jnp.where(in_first, first_listed, last_listed)
        masked = jnp.where(keep > 0.5, factor[node].astype(F32), 0.0).astype(BF16)
        own_masked[node] = masked
        lower[node, 0, z, x] = masked[:, :HALF]
        lower[node, 1, z, x] = masked[:, HALF:]

    pl.semaphore_wait(
        barrier, len(neighbours) + 2 * jnp.where(moves, 1, 0) + 2 * jnp.where(lower_moves, 1, 0)
    )

    def piece(node, half, first, second):
        return lower.at[node, half, second, first] if half == 0 else lower.at[node, half, first, second]

    def line(node, half, second):
        return lower.at[node, half, second] if half == 0 else lower.at[node, half, :, second]

    def line_part(node, half, second, part):
        where = pl.ds(2 * part, 2)
        return lower.at[node, half, second, where] if half == 0 else lower.at[node, half, where, second]

    axes = ("xz", "zx")

    def gather_copy(node, half, index, ref, axis, step):
        return start(
            ref, ref, gather_send.at[node, half, index], gather_recv.at[node, half, index], along(axis, step)
        )

    def first_phase(node):
        for half in range(2):
            a = axes[half][0]
            own = piece(node, half, coordinate[a], coordinate[axes[half][1]])
            copies[node, half, 0] = gather_copy(node, half, 0, own, a, 1)
            copies[node, half, 1] = gather_copy(node, half, 1, own, a, 3)

    def first_forward(node):
        for half in range(2):
            a, b = axes[half]
            for index, shift, step, cut in ((0, 3, 1, 0), (1, 1, 3, 128)):
                copies[node, half, index].wait_recv()
                got = piece(node, half, (coordinate[a] + shift) % 4, coordinate[b])
                copies[node, half, index + 2] = gather_copy(
                    node, half, index + 2, got.at[:, pl.ds(cut, 128)], a, step
                )

    def second_phase(node):
        for half in range(2):
            b = axes[half][1]
            copies[node, half, 2].wait_recv()
            copies[node, half, 3].wait_recv()
            own = line(node, half, coordinate[b])
            copies[node, half, 4] = gather_copy(node, half, 4, own, b, 1)
            copies[node, half, 5] = gather_copy(node, half, 5, own, b, 3)

    def second_forward(node):
        for half in range(2):
            b = axes[half][1]
            for index, shift, step, part in ((4, 3, 1, 0), (5, 1, 3, 1)):
                copies[node, half, index].wait_recv()
                got = line_part(node, half, (coordinate[b] + shift) % 4, part)
                copies[node, half, index + 2] = gather_copy(node, half, index + 2, got, b, step)

    def gathered(node, half):
        copies[node, half, 6].wait_recv()
        copies[node, half, 7].wait_recv()

    def multiply(node):
        for half in range(2):
            gathered(node, half)
            right = lower[node, half].reshape(ROWS, HALF)
            for part in range(4):
                rows = pl.ds(part * 192, 192)
                product = dot(inv_high[rows, :], right) + dot(inv_low[rows, :], right)
                partial[node, part, :, :, half * HALF : (half + 1) * HALF] = product.reshape(2, PIECE, HALF)
        copies["trade", node] = start(
            partial.at[node, :, 1 - core], traded.at[node], trade_sem.at[node, 0], trade_sem.at[node, 1], partner
        )

    def chain(later, earlier):
        g = pair_index(later, earlier)

        def body(part, carry):
            value = dot3(traded[earlier, part], couple_high[g], couple_low[g])
            correct[later, part] = value if earlier == 0 else correct[later, part] + value
            return carry

        lax.fori_loop(0, 4, body, 0)

    def reduce_start(node):
        copies["trade", node].wait_recv()
        total = traded[node] + partial[node, :, core]
        if node > 0:
            total = total + correct[node]
        traded[node] = -total
        for step in (1, 2, 3):
            at = pl.multiple_of((y + step) % 4 * QUARTER, QUARTER)
            copies["sum", node, step] = start(
                traded.at[node, :, :, pl.ds(at, QUARTER)], arrived.at[node, step - 1],
                sum_send.at[node, step - 1], sum_recv.at[node, step - 1], along("y", step),
            )

    def finish(node):
        at = pl.multiple_of(y * QUARTER, QUARTER)
        total = traded[node, :, :, pl.ds(at, QUARTER)]
        for step in (1, 2, 3):
            copies["sum", node, step].wait_recv()
            total = total + arrived[node, step - 1]
        solved[node, :, core] = total
        ref = solved.at[node, :, core]
        copies["swap", node] = start(ref, ref, swap_sem.at[node, 0], swap_sem.at[node, 1], partner)

    def rows_start(node):
        at = pl.multiple_of(y * QUARTER, QUARTER)
        where = (node, slice(None), pl.ds(at, QUARTER))
        for step in (1, 2, 3):
            copies["rows", node, step] = start(
                solved.at[node, (y + step) % 4, core], rows_out.at[where],
                rows_send.at[node, step - 1], rows_recv.at[node, step - 1], along("y", step),
            )
        rows_out[where] = solved[node, y, core]

    def columns_copy(node):
        return remote(
            rows_out.at[node], columns_out.at[node], columns_sem.at[node, 0], columns_sem.at[node, 1], forward
        )

    def columns_start(node):
        for step in (1, 2, 3):
            copies["rows", node, step].wait_recv()

        @pl.when(moves)
        def _():
            columns_copy(node).start()

        @pl.when(jnp.logical_not(moves))
        def _():
            columns_out[node] = rows_out[node]

    def columns_wait(node):
        @pl.when(moves)
        def _():
            columns_copy(node).wait()

    def lower_copy():
        return remote(
            own_masked, column_lower.at[:, z % 2, x], lower_sem.at[0], lower_sem.at[1], lower_to
        )

    def lower_start():
        @pl.when(lower_moves)
        def _():
            lower_copy().start()

        @pl.when(jnp.logical_not(lower_moves))
        def _():
            for node in range(NODES):
                column_lower[node, core, y] = own_masked[node]

    def lower_spread():
        @pl.when(lower_moves)
        def _():
            lower_copy().wait()

        ref = column_lower.at[:, core, y]
        for step in (1, 2, 3):
            copies["spread", step] = start(
                ref, ref, spread_send.at[step - 1], spread_recv.at[step - 1], along("y", step)
            )

    def lower_both():
        for step in (1, 2, 3):
            copies["spread", step].wait_recv()
        ref = column_lower.at[:, core]
        copies["both"] = start(ref, ref, both_sem.at[0], both_sem.at[1], partner)

    def prepare_tilde():
        copies["both"].wait_recv()
        for side_core in range(2):
            for part in range(4):
                rows = pl.ds((side_core * 4 + part) * PIECE, PIECE)
                for node in range(NODES):
                    own = column_lower[node, side_core, part]
                    if node == 0:
                        tilde_high[0, rows, :] = own
                        continue
                    first = column_lower[0, side_core, part]
                    g = pair_index(node, 0)
                    value = own.astype(F32) - (dot(first, couple_high[g]) + dot(first, couple_low[g]))
                    if node == 2:
                        high, low = tilde_high[1, rows, :], tilde_low[1, rows, :]
                        g = pair_index(2, 1)
                        value = value - (
                            dot(high, couple_high[g]) + dot(high, couple_low[g]) + dot(low, couple_high[g])
                        )
                    high, low = split(value)
                    tilde_high[node, rows, :] = high
                    tilde_low[node, rows, :] = low

    def inner_products(later):
        copies["swap", later].wait_recv()
        high, low = split(solved[later].reshape(COLS, QUARTER).T)
        mine = pl.ds(pl.multiple_of(core * HALF, HALF), HALF)
        for earlier in range(later + 1):
            right = tilde_high[earlier, :, mine]
            value = dot(high, right) + dot(low, right)
            if earlier > 0:
                value = value + dot(high, tilde_low[earlier, :, mine])
            for half in range(2):
                cut = value[:, half * QUARTER : (half + 1) * QUARTER]
                inner[half, first_block(later) + earlier] = -cut.reshape(4, 4, 8, QUARTER)

    def down_start(node, level):
        group = slice(first_block(node), first_block(node) + node + 1)
        for half in range(2):
            axis = ("xz", "zx")[half][level]
            for step in (1, 2, 3):
                target = (coordinate[axis] + step) % 4
                if level == 1:
                    src, dst = inner_sum.at[half, group, target], inner_last.at[half, step - 1, group]
                else:
                    src = inner.at[0, group, target] if half == 0 else inner.at[1, group, :, target]
                    dst = inner_recv.at[half, step - 1, group]
                sems = (node, level, half, step - 1)
                copies["down", node, level, half, step] = start(
                    src, dst, down_send.at[sems], down_recv.at[sems], along(axis, step)
                )

    def down_finish(node, level, half):
        group = slice(first_block(node), first_block(node) + node + 1)
        axis = ("xz", "zx")[half][level]
        own = coordinate[axis]
        if level == 1:
            total = inner_sum[half, group, own]
        else:
            total = inner[0, group, own] if half == 0 else inner[1, group, :, own]
        land = (inner_recv, inner_last)[level]
        for step in (1, 2, 3):
            copies["down", node, level, half, step].wait_recv()
            total = total + land[half, step - 1, group]
        return total

    def down_middle(node):
        group = slice(first_block(node), first_block(node) + node + 1)
        for half in range(2):
            inner_sum[half, group] = down_finish(node, 0, half)
        down_start(node, 1)

    def down_last(node):
        for half in range(2):
            total = down_finish(node, 1, half)
            lanes = pl.ds(pl.multiple_of(core * HALF + half * QUARTER, QUARTER), QUARTER)
            for earlier in range(node + 1):
                block = first_block(node) + earlier
                blocks_out[block, core, half, y, x, z] = tail[block, :, lanes] + total[earlier]

    orders = ("zxy", "yzx", "xyz")

    def up_ref(block, level, **other):
        done = orders[block % 3][:level]
        where = [other.get(a, slice(None) if a in done else coordinate[a]) for a in "yxz"]
        return blocks_out.at[(block, core, slice(None), *where)]

    def up_start(block, level):
        axis = orders[block % 3][level]
        ref = up_ref(block, level)
        for step in (1, 2, 3):
            sems = (block, level, step - 1)
            copies["up", block, level, step] = start(ref, ref, up_send.at[sems], up_recv.at[sems], along(axis, step))

    def up_wait(block, level):
        for step in (1, 2, 3):
            copies["up", block, level, step].wait_recv()

    def pair_start(block, step):
        axis = orders[block % 3][2]
        ref = up_ref(block, 2, **{axis: (coordinate[axis] - step) % 4})
        copies["pair", block, step] = start(ref, ref, pair_send.at[block, step], pair_recv.at[block, step], partner)

    def pair_rest(group):
        for step in (1, 3, 2):
            for block in group:
                copies["up", block, 2, step].wait_recv()
                pair_start(block, step)

    finished = pl.ds(pl.multiple_of(y * 128 + x * 32 + z * 8, 8), 8)

    def dot3_t(left, right_high, right_low):
        def across(a, b):
            return lax.dot_general(a, b, (((1,), (1,)), ((), ())), preferred_element_type=F32)

        high, low = split(left)
        return across(high, right_high) + across(high, right_low) + across(low, right_high)

    def split_diag(index):
        high, low = split(diag[index])
        side_high[...] = high
        side_low[...] = low

    def tail_terms():
        taken = []
        for g in range(3):
            side[...] = couple[g].T
            taken.append(side[finished, :])
        first, second, third = taken
        ch, cl = couple_high, couple_low
        mixed = dot3_t(third, ch[0], cl[0])
        stacked = jnp.concatenate([first, second, mixed], axis=0)
        split_diag(0)
        plain = dot3(stacked, side_high[...], side_low[...])
        turned = dot3_t(stacked, side_high[...], side_low[...])
        split_diag(1)
        after = dot3(third, side_high[...], side_low[...])
        after_t = dot3_t(third, side_high[...], side_low[...])
        a1, a2, a3 = plain[0:8], plain[8:16], plain[16:24]
        b1, b2, b3 = turned[0:8], turned[8:16], turned[16:24]
        through = dot3(jnp.concatenate([a1, a2, b3, a3], axis=0), ch[0], cl[0])
        e1, e2, e3, e4 = through[0:8], through[8:16], through[16:24], through[24:32]
        tail[0] = diag[0, finished, :]
        tail[1] = -b1
        tail[2] = diag[1, finished, :] + e1
        tail[3] = b3 - b2
        tail[4] = e2 - after_t - e3
        tail[5] = (
            diag[2, finished, :] + dot3(a2 - b3, ch[1], cl[1]) + dot3(after + e4 - e2, ch[2], cl[2])
        )

    for node in range(NODES):
        first_phase(node)
    lower_start()
    first_forward(0)
    second_phase(0)
    first_forward(1)
    first_forward(2)
    load_inv.wait()
    for block in range(6):
        where = slice(block * 256, (block + 1) * 256)
        high, low = split(inv[where, :].T)
        inv_high[:, where] = high
        inv_low[:, where] = low
    second_forward(0)
    second_phase(1)
    lower_spread()
    load_couple.wait()
    load_diag.wait()
    for g in range(3):
        high, low = split(couple[g])
        couple_high[g] = high
        couple_low[g] = low
    multiply(0)
    second_forward(1)
    second_phase(2)
    reduce_start(0)
    chain(1, 0)
    multiply(1)
    second_forward(2)
    lower_both()
    reduce_start(1)
    chain(2, 0)
    chain(2, 1)
    finish(0)
    rows_start(0)
    multiply(2)
    prepare_tilde()
    reduce_start(2)
    inner_products(0)
    down_start(0, 0)
    finish(1)
    rows_start(1)
    inner_products(1)
    down_start(1, 0)
    columns_start(0)
    tail_terms()
    down_middle(0)
    down_middle(1)
    columns_start(1)
    down_last(0)
    down_last(1)
    for block in (0, 1, 2):
        up_start(block, 0)
    finish(2)
    rows_start(2)
    inner_products(2)
    down_start(2, 0)
    for block in (0, 1, 2):
        up_wait(block, 0)
        up_start(block, 1)
    down_middle(2)
    columns_start(2)
    for block in (0, 1, 2):
        up_wait(block, 1)
        up_start(block, 2)
        pair_start(block, 0)
    down_last(2)
    for block in (3, 4, 5):
        up_start(block, 0)
    for block in (3, 4, 5):
        up_wait(block, 0)
        up_start(block, 1)
    for block in (3, 4, 5):
        up_wait(block, 1)
        up_start(block, 2)
        pair_start(block, 0)
    pair_rest((0, 1, 2))
    pair_rest((3, 4, 5))
    for block in range(6):
        for step in range(4):
            copies["pair", block, step].wait_recv()
    for node in range(NODES):
        columns_wait(node)
    for copy in sent:
        copy.wait_send()


def fused(ancestor_inverse, factor, coupling, diagonal_inverse, ancestors):
    vmem = pl.BlockSpec(memory_space=pltpu.VMEM)
    hbm = pl.BlockSpec(memory_space=pl.ANY)
    dma = pltpu.SemaphoreType.DMA
    square = (SN, SN)
    return pl.pallas_call(
        kernel,
        out_shape=(
            jax.ShapeDtypeStruct((NODES, PIECE, SN), F32),
            jax.ShapeDtypeStruct((NODES, PIECE, SN), F32),
            jax.ShapeDtypeStruct((6, 2, 2, 4, 4, 4, 8, QUARTER), F32),
        ),
        in_specs=[hbm, vmem, hbm, hbm, pl.BlockSpec(memory_space=pltpu.SMEM)],
        out_specs=(vmem, vmem, vmem),
        scratch_shapes=[
            pltpu.VMEM((ROWS, COLS), F32),
            pltpu.VMEM((COLS, ROWS), BF16),
            pltpu.VMEM((COLS, ROWS), BF16),
            pltpu.VMEM((NODES, PIECE, SN), BF16),
            pltpu.VMEM((NODES, 2, 4, 4, PIECE, HALF), BF16),
            pltpu.VMEM((NODES, 4, 2, PIECE, SN), F32),
            pltpu.VMEM((NODES, 4, PIECE, SN), F32),
            pltpu.VMEM((NODES, 4, PIECE, SN), F32),
            pltpu.VMEM((NODES, 3, 4, PIECE, QUARTER), F32),
            pltpu.VMEM((NODES, 4, 2, PIECE, QUARTER), F32),
            pltpu.VMEM((3,) + square, F32),
            pltpu.VMEM((3,) + square, BF16),
            pltpu.VMEM((3,) + square, BF16),
            pltpu.VMEM((3,) + square, F32),
            pltpu.VMEM((6, 8, SN), F32),
            pltpu.VMEM(square, F32),
            pltpu.VMEM(square, BF16),
            pltpu.VMEM(square, BF16),
            pltpu.VMEM((NODES, 2, 4, PIECE, SN), BF16),
            pltpu.VMEM((NODES, COLS, SN), BF16),
            pltpu.VMEM((NODES, COLS, SN), BF16),
            pltpu.VMEM((2, 6, 4, 4, 8, QUARTER), F32),
            pltpu.VMEM((2, 3, 6, 4, 8, QUARTER), F32),
            pltpu.VMEM((2, 6, 4, 8, QUARTER), F32),
            pltpu.VMEM((2, 3, 6, 8, QUARTER), F32),
            dma((3,)),
            dma((NODES, 2, 8)),
            dma((NODES, 2, 8)),
            dma((2,)),
            dma((3,)),
            dma((3,)),
            dma((2,)),
            dma((NODES, 2)),
            dma((NODES, 2)),
            dma((NODES, 3)),
            dma((NODES, 3)),
            dma((NODES, 3)),
            dma((NODES, 3)),
            dma((NODES, 2)),
            dma((NODES, 2, 2, 3)),
            dma((NODES, 2, 2, 3)),
            dma((6, 3, 3)),
            dma((6, 3, 3)),
            dma((6, 4)),
            dma((6, 4)),
        ],
        compiler_params=pltpu.CompilerParams(
            collective_id=0, has_side_effects=True, vmem_limit_bytes=63 << 20
        ),
        name="selected_inversion",
    )(ancestor_inverse, factor, coupling, diagonal_inverse, ancestors)


def assemble_kernel(blocks, rows, columns, out, rows_out, columns_out):
    first, second = pl.program_id(0), pl.program_id(1)
    later, earlier = jnp.maximum(first, second), jnp.minimum(first, second)
    block = later * (later + 1) // 2 + earlier

    def lanes(half):
        return blocks[block, half // 2, half % 2].reshape(SN, QUARTER)

    @pl.when(jnp.logical_and(first == 0, second == 0))
    def _():
        rows_out[...] = rows[...]
        columns_out[...] = columns[...]

    @pl.when(first >= second)
    def _():
        for half in range(4):
            out[0, 0, :, half * QUARTER : (half + 1) * QUARTER] = lanes(half)

    @pl.when(first < second)
    def _():
        for half in range(4):
            out[0, 0, half * QUARTER : (half + 1) * QUARTER, :] = lanes(half).T


def assemble(blocks, rows, columns):
    whole = pl.BlockSpec(memory_space=pltpu.VMEM)
    return pl.pallas_call(
        assemble_kernel,
        out_shape=(
            jax.ShapeDtypeStruct((NODES, NODES, SN, SN), F32),
            jax.ShapeDtypeStruct(rows.shape, F32),
            jax.ShapeDtypeStruct(columns.shape, F32),
        ),
        grid=(NODES, NODES),
        in_specs=[whole, whole, whole],
        out_specs=(
            pl.BlockSpec((1, 1, SN, SN), lambda first, second: (first, second, 0, 0)),
            pl.BlockSpec(rows.shape, lambda first, second: (0, 0, 0)),
            pl.BlockSpec(columns.shape, lambda first, second: (0, 0, 0)),
        ),
        compiler_params=pltpu.CompilerParams(vmem_limit_bytes=24 << 20),
        name="assemble_node_blocks",
    )(blocks, rows, columns)


def local(ancestor_inverse, factor, coupling, diagonal_inverse, ancestors):
    block_rows, block_columns, blocks = fused(
        ancestor_inverse, factor, coupling, diagonal_inverse, ancestors
    )
    node_blocks, block_rows, block_columns = assemble(blocks, block_rows, block_columns)
    return block_columns, block_rows, node_blocks


def solution(mesh):
    placed = (P("row", "col"), P(None, ("row", "col"), None), P(), P(), P())
    return jax.shard_map(
        local,
        mesh=mesh,
        in_specs=placed,
        out_specs=(P(None, ("row", "col"), None), P(None, ("col", "row"), None), P()),
        check_vma=False,
    )
```

```python
import jax
import jax.numpy as jnp
from jax import lax
from jax.experimental import pallas as pl
from jax.experimental.pallas import tpu as pltpu
from jax.sharding import PartitionSpec as P

MESH = pl.DeviceIdType.MESH
F32 = jnp.float32
BF16 = jnp.bfloat16
NODES = 3
SN = 512
HALF = 256
PIECE = 96
ROWS = 1536
COLS = 768
QUARTER = 128


def pair_index(later, earlier):
    return later * (later - 1) // 2 + earlier


def split(value):
    high = value.astype(BF16)
    return high, (value - high.astype(F32)).astype(BF16)


def dot(left, right):
    return jnp.dot(left, right, preferred_element_type=F32)


def dot3(left, right_high, right_low):
    high, low = split(left)
    return dot(high, right_high) + dot(high, right_low) + dot(low, right_high)


def first_block(node):
    return node * (node + 1) // 2


def kernel(
    inverse, factor, coupling, diagonal, ancestors,
    rows_out, columns_out, blocks_out,
    inv, inv_high, inv_low, own_masked, lower, partial, traded, correct, relay, outgoing, arrived, solved,
    couple, couple_high, couple_low, diag, tail, side, side_high, side_low,
    column_lower, tilde_high, tilde_low, inner, inner_recv, inner_sum, inner_last,
    local_sem, gather_send, gather_recv, lower_sem, spread_send, spread_recv, both_sem, columns_sem, trade_sem,
    sum_send, sum_recv, rows_send, rows_recv, swap_sem, down_send, down_recv, up_send, up_recv, pair_send, pair_recv,
):
    row = lax.axis_index("row")
    col = lax.axis_index("col")
    y, core, z, x = row // 2, row % 2, col // 4, col % 4

    def device(dy=0, dcore=0, dz=0, dx=0):
        return (
            ((y + dy) % 4) * 2 + (core + dcore) % 2,
            ((z + dz) % 4) * 4 + (x + dx) % 4,
        )

    def along(axis, step):
        return device(**{"d" + axis: step % 4})

    coordinate = {"x": x, "y": y, "z": z}
    partner = device(dcore=1)
    forward = (col // 2, (col % 2) * 8 + row)
    backward = (col % 8, 2 * row + col // 8)
    moves = jnp.logical_or(forward[0] != row, forward[1] != col)
    lower_to = (x * 2 + z % 2, y * 4 + 2 * core + z // 2)
    lower_from = (z * 2 + x // 2, (2 * (x % 2) + core) * 4 + y)
    lower_moves = jnp.logical_or(lower_to[0] != row, lower_to[1] != col)

    sent = []
    copies = {}

    def remote(src, dst, send_sem, recv_sem, target):
        return pltpu.make_async_remote_copy(
            src_ref=src, dst_ref=dst, send_sem=send_sem, recv_sem=recv_sem,
            device_id=target, device_id_type=MESH,
        )

    def start(src, dst, send_sem, recv_sem, target):
        copy = remote(src, dst, send_sem, recv_sem, target)
        copy.start()
        sent.append(copy)
        return copy

    barrier = pltpu.get_barrier_semaphore()
    neighbours = [along(a, s) for a in "xyz" for s in (1, 2, 3)] + [partner]
    for target in neighbours:
        pl.semaphore_signal(barrier, inc=1, device_id=target, device_id_type=MESH)

    @pl.when(moves)
    def _():
        for target in (forward, backward):
            pl.semaphore_signal(barrier, inc=1, device_id=target, device_id_type=MESH)

    @pl.when(lower_moves)
    def _():
        for target in (lower_to, lower_from):
            pl.semaphore_signal(barrier, inc=1, device_id=target, device_id_type=MESH)

    load_inv = pltpu.make_async_copy(inverse, inv, local_sem.at[0])
    load_couple = pltpu.make_async_copy(coupling, couple, local_sem.at[1])
    load_diag = pltpu.make_async_copy(diagonal, diag, local_sem.at[2])
    load_inv.start()
    load_couple.start()
    load_diag.start()

    first_row = (row * 16 + col) * PIECE
    block_first = first_row // SN
    block_last = (first_row + PIECE - 1) // SN
    row_at = first_row + lax.broadcasted_iota(jnp.int32, (PIECE, SN), 0)
    in_first = row_at < (block_first + 1) * SN
    for node in range(NODES):
        first_listed = jnp.float32(0)
        last_listed = jnp.float32(0)
        for slot in range(24):
            entry = ancestors[node, slot]
            first_listed = jnp.where(entry == block_first, 1.0, first_listed)
            last_listed = jnp.where(entry == block_last, 1.0, last_listed)
        keep = jnp.where(in_first, first_listed, last_listed)
        masked = jnp.where(keep > 0.5, factor[node].astype(F32), 0.0).astype(BF16)
        own_masked[node] = masked
        lower[node, 0, z, x] = masked[:, :HALF]
        lower[node, 1, z, x] = masked[:, HALF:]

    pl.semaphore_wait(
        barrier, len(neighbours) + 2 * jnp.where(moves, 1, 0) + 2 * jnp.where(lower_moves, 1, 0)
    )

    def piece(node, half, first, second):
        return lower.at[node, half, second, first] if half == 0 else lower.at[node, half, first, second]

    def line(node, half, second):
        return lower.at[node, half, second] if half == 0 else lower.at[node, half, :, second]

    def line_part(node, half, second, part):
        where = pl.ds(2 * part, 2)
        return lower.at[node, half, second, where] if half == 0 else lower.at[node, half, where, second]

    axes = ("xz", "zx")

    def gather_copy(node, half, index, ref, axis, step):
        return start(
            ref, ref, gather_send.at[node, half, index], gather_recv.at[node, half, index], along(axis, step)
        )

    def first_phase(node):
        for half in range(2):
            a = axes[half][0]
            own = piece(node, half, coordinate[a], coordinate[axes[half][1]])
            copies[node, half, 0] = gather_copy(node, half, 0, own, a, 1)
            copies[node, half, 1] = gather_copy(node, half, 1, own, a, 3)

    def first_forward(node):
        for half in range(2):
            a, b = axes[half]
            for index, shift, step, cut in ((0, 3, 1, 0), (1, 1, 3, 128)):
                copies[node, half, index].wait_recv()
                got = piece(node, half, (coordinate[a] + shift) % 4, coordinate[b])
                copies[node, half, index + 2] = gather_copy(
                    node, half, index + 2, got.at[:, pl.ds(cut, 128)], a, step
                )

    def second_phase(node):
        for half in range(2):
            b = axes[half][1]
            copies[node, half, 2].wait_recv()
            copies[node, half, 3].wait_recv()
            own = line(node, half, coordinate[b])
            copies[node, half, 4] = gather_copy(node, half, 4, own, b, 1)
            copies[node, half, 5] = gather_copy(node, half, 5, own, b, 3)

    def second_forward(node):
        for half in range(2):
            b = axes[half][1]
            for index, shift, step, part in ((4, 3, 1, 0), (5, 1, 3, 1)):
                copies[node, half, index].wait_recv()
                got = line_part(node, half, (coordinate[b] + shift) % 4, part)
                copies[node, half, index + 2] = gather_copy(node, half, index + 2, got, b, step)

    def gathered(node, half):
        copies[node, half, 6].wait_recv()
        copies[node, half, 7].wait_recv()

    def multiply(node):
        for half in range(2):
            gathered(node, half)
            right = lower[node, half].reshape(ROWS, HALF)
            for part in range(4):
                rows = pl.ds(part * 192, 192)
                product = dot(inv_high[rows, :], right) + dot(inv_low[rows, :], right)
                partial[node, part, :, :, half * HALF : (half + 1) * HALF] = product.reshape(2, PIECE, HALF)
        copies["trade", node] = start(
            partial.at[node, :, 1 - core], traded.at[node], trade_sem.at[node, 0], trade_sem.at[node, 1], partner
        )

    def chain(later, earlier):
        g = pair_index(later, earlier)

        def body(part, carry):
            value = dot3(traded[earlier, part], couple_high[g], couple_low[g])
            correct[later, part] = value if earlier == 0 else correct[later, part] + value
            return carry

        lax.fori_loop(0, 4, body, 0)

    def reduce_start(node):
        copies["trade", node].wait_recv()
        total = traded[node] + partial[node, :, core]
        if node > 0:
            total = total + correct[node]
        traded[node] = -total
        for way, step in ((0, 1), (1, 3)):
            copies["relay", node, way] = start(
                traded.at[node, pl.ds(2 * way, 2), :, quarter(2)], relay.at[node, way],
                sum_send.at[node, way], sum_recv.at[node, way], along("y", step),
            )

    def quarter(step):
        return pl.ds(pl.multiple_of((y + step) % 4 * QUARTER, QUARTER), QUARTER)

    def reduce_relay(node):
        for way, step in ((0, 1), (1, 3)):
            copies["relay", node, way].wait_recv()
            with_relay, plain = (slice(0, 2), slice(2, 4)) if way == 0 else (slice(2, 4), slice(0, 2))
            outgoing[node, way, with_relay] = traded[node, with_relay, :, quarter(step)] + relay[node, way]
            outgoing[node, way, plain] = traded[node, plain, :, quarter(step)]
            copies["sum", node, way] = start(
                outgoing.at[node, way], arrived.at[node, way],
                sum_send.at[node, 2 + way], sum_recv.at[node, 2 + way], along("y", step),
            )

    def finish(node):
        total = traded[node, :, :, quarter(0)]
        for way in range(2):
            copies["sum", node, way].wait_recv()
            total = total + arrived[node, way]
        solved[node, :, core] = total
        ref = solved.at[node, :, core]
        copies["swap", node] = start(ref, ref, swap_sem.at[node, 0], swap_sem.at[node, 1], partner)

    def rows_start(node):
        at = pl.multiple_of(y * QUARTER, QUARTER)
        where = (node, slice(None), pl.ds(at, QUARTER))
        for step in (1, 2, 3):
            copies["rows", node, step] = start(
                solved.at[node, (y + step) % 4, core], rows_out.at[where],
                rows_send.at[node, step - 1], rows_recv.at[node, step - 1], along("y", step),
            )
        rows_out[where] = solved[node, y, core]

    def columns_copy(node):
        return remote(
            rows_out.at[node], columns_out.at[node], columns_sem.at[node, 0], columns_sem.at[node, 1], forward
        )

    def columns_start(node):
        for step in (1, 2, 3):
            copies["rows", node, step].wait_recv()

        @pl.when(moves)
        def _():
            columns_copy(node).start()

        @pl.when(jnp.logical_not(moves))
        def _():
            columns_out[node] = rows_out[node]

    def columns_wait(node):
        @pl.when(moves)
        def _():
            columns_copy(node).wait()

    def lower_copy():
        return remote(
            own_masked, column_lower.at[:, z % 2, x], lower_sem.at[0], lower_sem.at[1], lower_to
        )

    def lower_start():
        @pl.when(lower_moves)
        def _():
            lower_copy().start()

        @pl.when(jnp.logical_not(lower_moves))
        def _():
            for node in range(NODES):
                column_lower[node, core, y] = own_masked[node]

    def lower_spread():
        @pl.when(lower_moves)
        def _():
            lower_copy().wait()

        ref = column_lower.at[:, core, y]
        for way, step in ((0, 1), (1, 3)):
            copies["spread", way] = start(ref, ref, spread_send.at[way], spread_recv.at[way], along("y", step))

    def lower_relay():
        for way, step in ((0, 1), (1, 3)):
            copies["spread", way].wait_recv()
            ref = column_lower.at[:, core, (y + 4 - step) % 4, :, pl.ds(way * HALF, HALF)]
            copies["spread", 2 + way] = start(
                ref, ref, spread_send.at[2 + way], spread_recv.at[2 + way], along("y", step)
            )

    def lower_both():
        for way in range(2):
            copies["spread", 2 + way].wait_recv()
        ref = column_lower.at[:, core]
        copies["both"] = start(ref, ref, both_sem.at[0], both_sem.at[1], partner)

    def prepare_tilde():
        copies["both"].wait_recv()
        for side_core in range(2):
            for part in range(4):
                rows = pl.ds((side_core * 4 + part) * PIECE, PIECE)
                for node in range(NODES):
                    own = column_lower[node, side_core, part]
                    if node == 0:
                        tilde_high[0, rows, :] = own
                        continue
                    first = column_lower[0, side_core, part]
                    g = pair_index(node, 0)
                    value = own.astype(F32) - (dot(first, couple_high[g]) + dot(first, couple_low[g]))
                    if node == 2:
                        high, low = tilde_high[1, rows, :], tilde_low[1, rows, :]
                        g = pair_index(2, 1)
                        value = value - (
                            dot(high, couple_high[g]) + dot(high, couple_low[g]) + dot(low, couple_high[g])
                        )
                    high, low = split(value)
                    tilde_high[node, rows, :] = high
                    tilde_low[node, rows, :] = low

    def inner_products(later):
        copies["swap", later].wait_recv()
        high, low = split(solved[later].reshape(COLS, QUARTER).T)
        mine = pl.ds(pl.multiple_of(core * HALF, HALF), HALF)
        for earlier in range(later + 1):
            right = tilde_high[earlier, :, mine]
            value = dot(high, right) + dot(low, right)
            if earlier > 0:
                value = value + dot(high, tilde_low[earlier, :, mine])
            for half in range(2):
                cut = value[:, half * QUARTER : (half + 1) * QUARTER]
                inner[half, first_block(later) + earlier] = -cut.reshape(4, 4, 8, QUARTER)

    def down_start(node, level):
        group = slice(first_block(node), first_block(node) + node + 1)
        for half in range(2):
            axis = ("xz", "zx")[half][level]
            for step in (1, 2, 3):
                target = (coordinate[axis] + step) % 4
                if level == 1:
                    src, dst = inner_sum.at[half, group, target], inner_last.at[half, step - 1, group]
                else:
                    src = inner.at[0, group, target] if half == 0 else inner.at[1, group, :, target]
                    dst = inner_recv.at[half, step - 1, group]
                sems = (node, level, half, step - 1)
                copies["down", node, level, half, step] = start(
                    src, dst, down_send.at[sems], down_recv.at[sems], along(axis, step)
                )

    def down_finish(node, level, half):
        group = slice(first_block(node), first_block(node) + node + 1)
        axis = ("xz", "zx")[half][level]
        own = coordinate[axis]
        if level == 1:
            total = inner_sum[half, group, own]
        else:
            total = inner[0, group, own] if half == 0 else inner[1, group, :, own]
        land = (inner_recv, inner_last)[level]
        for step in (1, 2, 3):
            copies["down", node, level, half, step].wait_recv()
            total = total + land[half, step - 1, group]
        return total

    def down_middle(node):
        group = slice(first_block(node), first_block(node) + node + 1)
        for half in range(2):
            inner_sum[half, group] = down_finish(node, 0, half)
        down_start(node, 1)

    def down_last(node):
        for half in range(2):
            total = down_finish(node, 1, half)
            lanes = pl.ds(pl.multiple_of(core * HALF + half * QUARTER, QUARTER), QUARTER)
            for earlier in range(node + 1):
                block = first_block(node) + earlier
                blocks_out[block, core, half, y, x, z] = tail[block, :, lanes] + total[earlier]

    orders = ("yxz", "yzx", "yxz", "zxy", "yzx", "xyz")

    def up_ref(block, level, **other):
        done = orders[block][:level]
        where = [other.get(a, slice(None) if a in done else coordinate[a]) for a in "yxz"]
        return blocks_out.at[(block, core, slice(None), *where)]

    def up_start(block, level):
        axis = orders[block][level]
        ref = up_ref(block, level)
        for step in (1, 2, 3):
            sems = (block, level, step - 1)
            copies["up", block, level, step] = start(ref, ref, up_send.at[sems], up_recv.at[sems], along(axis, step))

    def up_wait(block, level):
        for step in (1, 2, 3):
            copies["up", block, level, step].wait_recv()

    def pair_start(block, step):
        axis = orders[block][2]
        ref = up_ref(block, 2, **{axis: (coordinate[axis] - step) % 4})
        copies["pair", block, step] = start(ref, ref, pair_send.at[block, step], pair_recv.at[block, step], partner)

    def pair_rest(group):
        for step in (1, 3, 2):
            for block in group:
                copies["up", block, 2, step].wait_recv()
                pair_start(block, step)

    finished = pl.ds(pl.multiple_of(y * 128 + x * 32 + z * 8, 8), 8)

    def dot3_t(left, right_high, right_low):
        def across(a, b):
            return lax.dot_general(a, b, (((1,), (1,)), ((), ())), preferred_element_type=F32)

        high, low = split(left)
        return across(high, right_high) + across(high, right_low) + across(low, right_high)

    def split_diag(index):
        high, low = split(diag[index])
        side_high[...] = high
        side_low[...] = low

    def tail_terms():
        taken = []
        for g in range(3):
            side[...] = couple[g].T
            taken.append(side[finished, :])
        first, second, third = taken
        ch, cl = couple_high, couple_low
        mixed = dot3_t(third, ch[0], cl[0])
        stacked = jnp.concatenate([first, second, mixed], axis=0)
        split_diag(0)
        plain = dot3(stacked, side_high[...], side_low[...])
        turned = dot3_t(stacked, side_high[...], side_low[...])
        split_diag(1)
        after = dot3(third, side_high[...], side_low[...])
        after_t = dot3_t(third, side_high[...], side_low[...])
        a1, a2, a3 = plain[0:8], plain[8:16], plain[16:24]
        b1, b2, b3 = turned[0:8], turned[8:16], turned[16:24]
        through = dot3(jnp.concatenate([a1, a2, b3, a3], axis=0), ch[0], cl[0])
        e1, e2, e3, e4 = through[0:8], through[8:16], through[16:24], through[24:32]
        tail[0] = diag[0, finished, :]
        tail[1] = -b1
        tail[2] = diag[1, finished, :] + e1
        tail[3] = b3 - b2
        tail[4] = e2 - after_t - e3
        tail[5] = (
            diag[2, finished, :] + dot3(a2 - b3, ch[1], cl[1]) + dot3(after + e4 - e2, ch[2], cl[2])
        )

    for node in range(NODES):
        first_phase(node)
    lower_start()
    first_forward(0)
    second_phase(0)
    first_forward(1)
    first_forward(2)
    load_inv.wait()
    for block in range(6):
        where = slice(block * 256, (block + 1) * 256)
        high, low = split(inv[where, :].T)
        inv_high[:, where] = high
        inv_low[:, where] = low
    second_forward(0)
    second_phase(1)
    lower_spread()
    load_couple.wait()
    load_diag.wait()
    for g in range(3):
        high, low = split(couple[g])
        couple_high[g] = high
        couple_low[g] = low
    multiply(0)
    second_forward(1)
    second_phase(2)
    lower_relay()
    reduce_start(0)
    chain(1, 0)
    multiply(1)
    second_forward(2)
    reduce_relay(0)
    reduce_start(1)
    lower_both()
    chain(2, 0)
    chain(2, 1)
    reduce_relay(1)
    finish(0)
    rows_start(0)
    multiply(2)
    reduce_start(2)
    prepare_tilde()
    reduce_relay(2)
    inner_products(0)
    down_start(0, 0)
    finish(1)
    rows_start(1)
    inner_products(1)
    down_start(1, 0)
    columns_start(0)
    tail_terms()
    down_middle(0)
    down_middle(1)
    columns_start(1)
    down_last(0)
    down_last(1)
    for block in (0, 1, 2):
        up_start(block, 0)
    finish(2)
    rows_start(2)
    inner_products(2)
    down_start(2, 0)
    for block in (0, 1, 2):
        up_wait(block, 0)
        up_start(block, 1)
    down_middle(2)
    columns_start(2)
    for block in (0, 1, 2):
        up_wait(block, 1)
        up_start(block, 2)
        pair_start(block, 0)
    down_last(2)
    for block in (3, 4, 5):
        up_start(block, 0)
    for block in (3, 4, 5):
        up_wait(block, 0)
        up_start(block, 1)
    for block in (3, 4, 5):
        up_wait(block, 1)
        up_start(block, 2)
        pair_start(block, 0)
    pair_rest((0, 1, 2))
    pair_rest((3, 4, 5))
    for block in range(6):
        for step in range(4):
            copies["pair", block, step].wait_recv()
    for node in range(NODES):
        columns_wait(node)
    for copy in sent:
        copy.wait_send()


def fused(ancestor_inverse, factor, coupling, diagonal_inverse, ancestors):
    vmem = pl.BlockSpec(memory_space=pltpu.VMEM)
    hbm = pl.BlockSpec(memory_space=pl.ANY)
    dma = pltpu.SemaphoreType.DMA
    square = (SN, SN)
    return pl.pallas_call(
        kernel,
        out_shape=(
            jax.ShapeDtypeStruct((NODES, PIECE, SN), F32),
            jax.ShapeDtypeStruct((NODES, PIECE, SN), F32),
            jax.ShapeDtypeStruct((6, 2, 2, 4, 4, 4, 8, QUARTER), F32),
        ),
        in_specs=[hbm, vmem, hbm, hbm, pl.BlockSpec(memory_space=pltpu.SMEM)],
        out_specs=(vmem, vmem, vmem),
        scratch_shapes=[
            pltpu.VMEM((ROWS, COLS), F32),
            pltpu.VMEM((COLS, ROWS), BF16),
            pltpu.VMEM((COLS, ROWS), BF16),
            pltpu.VMEM((NODES, PIECE, SN), BF16),
            pltpu.VMEM((NODES, 2, 4, 4, PIECE, HALF), BF16),
            pltpu.VMEM((NODES, 4, 2, PIECE, SN), F32),
            pltpu.VMEM((NODES, 4, PIECE, SN), F32),
            pltpu.VMEM((NODES, 4, PIECE, SN), F32),
            pltpu.VMEM((NODES, 2, 2, PIECE, QUARTER), F32),
            pltpu.VMEM((NODES, 2, 4, PIECE, QUARTER), F32),
            pltpu.VMEM((NODES, 2, 4, PIECE, QUARTER), F32),
            pltpu.VMEM((NODES, 4, 2, PIECE, QUARTER), F32),
            pltpu.VMEM((3,) + square, F32),
            pltpu.VMEM((3,) + square, BF16),
            pltpu.VMEM((3,) + square, BF16),
            pltpu.VMEM((3,) + square, F32),
            pltpu.VMEM((6, 8, SN), F32),
            pltpu.VMEM(square, F32),
            pltpu.VMEM(square, BF16),
            pltpu.VMEM(square, BF16),
            pltpu.VMEM((NODES, 2, 4, PIECE, SN), BF16),
            pltpu.VMEM((NODES, COLS, SN), BF16),
            pltpu.VMEM((NODES, COLS, SN), BF16),
            pltpu.VMEM((2, 6, 4, 4, 8, QUARTER), F32),
            pltpu.VMEM((2, 3, 6, 4, 8, QUARTER), F32),
            pltpu.VMEM((2, 6, 4, 8, QUARTER), F32),
            pltpu.VMEM((2, 3, 6, 8, QUARTER), F32),
            dma((3,)),
            dma((NODES, 2, 8)),
            dma((NODES, 2, 8)),
            dma((2,)),
            dma((4,)),
            dma((4,)),
            dma((2,)),
            dma((NODES, 2)),
            dma((NODES, 2)),
            dma((NODES, 4)),
            dma((NODES, 4)),
            dma((NODES, 3)),
            dma((NODES, 3)),
            dma((NODES, 2)),
            dma((NODES, 2, 2, 3)),
            dma((NODES, 2, 2, 3)),
            dma((6, 3, 3)),
            dma((6, 3, 3)),
            dma((6, 4)),
            dma((6, 4)),
        ],
        compiler_params=pltpu.CompilerParams(
            collective_id=0, has_side_effects=True, vmem_limit_bytes=63 << 20
        ),
        name="selected_inversion",
    )(ancestor_inverse, factor, coupling, diagonal_inverse, ancestors)


def block_at(step):
    return jnp.where(step > 1, step - 1, step) - jnp.where(step > 4, 1, 0) - jnp.where(step > 6, 1, 0)


def place_at(step):
    turned = jnp.logical_or(step == 2, jnp.logical_or(step == 5, step == 7))
    later = jnp.where(step > 3, 2, jnp.where(step > 0, 1, 0))
    earlier = jnp.where(step == 8, 2, jnp.where(jnp.logical_or(step == 3, step // 2 == 3), 1, 0))
    return turned, jnp.where(turned, earlier, later), jnp.where(turned, later, earlier)


def assemble_kernel(block, rows, columns, out, rows_out, columns_out, sems):
    step = pl.program_id(0)
    turned = place_at(step)[0]

    def copies():
        return (
            pltpu.make_async_copy(rows, rows_out, sems.at[0]),
            pltpu.make_async_copy(columns, columns_out, sems.at[1]),
        )

    def lanes(half):
        return block[0, half // 2, half % 2].reshape(SN, QUARTER)

    @pl.when(step == 0)
    def _():
        for copy in copies():
            copy.start()

    @pl.when(jnp.logical_not(turned))
    def _():
        for half in range(4):
            out[0, 0, :, half * QUARTER : (half + 1) * QUARTER] = lanes(half)

    @pl.when(turned)
    def _():
        for half in range(4):
            out[0, 0, half * QUARTER : (half + 1) * QUARTER, :] = lanes(half).T

    @pl.when(step == 8)
    def _():
        for copy in copies():
            copy.wait()


def assemble(blocks, rows, columns):
    hbm = pl.BlockSpec(memory_space=pl.ANY)
    return pl.pallas_call(
        assemble_kernel,
        out_shape=(
            jax.ShapeDtypeStruct((NODES, NODES, SN, SN), F32),
            jax.ShapeDtypeStruct(rows.shape, F32),
            jax.ShapeDtypeStruct(columns.shape, F32),
        ),
        grid=(9,),
        in_specs=[
            pl.BlockSpec((1, 2, 2, 4, 4, 4, 8, QUARTER), lambda step: (block_at(step),) + (0,) * 7), hbm, hbm
        ],
        out_specs=(
            pl.BlockSpec((1, 1, SN, SN), lambda step: place_at(step)[1:] + (0, 0)), hbm, hbm
        ),
        scratch_shapes=[pltpu.SemaphoreType.DMA((2,))],
        compiler_params=pltpu.CompilerParams(vmem_limit_bytes=60 << 20),
        name="assemble_node_blocks",
    )(blocks, rows, columns)


def local(ancestor_inverse, factor, coupling, diagonal_inverse, ancestors):
    block_rows, block_columns, blocks = fused(
        ancestor_inverse, factor, coupling, diagonal_inverse, ancestors
    )
    node_blocks, block_rows, block_columns = assemble(blocks, block_rows, block_columns)
    return block_columns, block_rows, node_blocks


def solution(mesh):
    placed = (P("row", "col"), P(None, ("row", "col"), None), P(), P(), P())
    return jax.shard_map(
        local,
        mesh=mesh,
        in_specs=placed,
        out_specs=(P(None, ("row", "col"), None), P(None, ("col", "row"), None), P()),
        check_vma=False,
    )
```

```python
import jax
import jax.numpy as jnp
from jax import lax
from jax.experimental import pallas as pl
from jax.experimental.pallas import tpu as pltpu
from jax.sharding import PartitionSpec as P

MESH = pl.DeviceIdType.MESH
F32 = jnp.float32
BF16 = jnp.bfloat16
NODES = 3
SN = 512
HALF = 256
PIECE = 96
ROWS = 1536
COLS = 768
QUARTER = 128


def pair_index(later, earlier):
    return later * (later - 1) // 2 + earlier


def split(value):
    high = value.astype(BF16)
    return high, (value - high.astype(F32)).astype(BF16)


def dot(left, right):
    return jnp.dot(left, right, preferred_element_type=F32)


def dot3(left, right_high, right_low):
    high, low = split(left)
    return dot(high, right_high) + dot(high, right_low) + dot(low, right_high)


def first_block(node):
    return node * (node + 1) // 2


def kernel(
    inverse, factor, coupling, diagonal, ancestors,
    rows_out, columns_out, blocks_out,
    inv, inv_high, inv_low, own_masked, lower, partial, traded, correct, relay, outgoing, arrived, solved,
    couple, couple_high, couple_low, diag, tail, side, side_high, side_low,
    column_lower, tilde_high, tilde_low, inner, inner_recv, inner_sum, inner_last,
    local_sem, gather_send, gather_recv, lower_sem, spread_send, spread_recv, both_sem, columns_sem, trade_sem,
    sum_send, sum_recv, rows_send, rows_recv, swap_sem, down_send, down_recv, up_send, up_recv, pair_send, pair_recv,
):
    row = lax.axis_index("row")
    col = lax.axis_index("col")
    y, core, z, x = row // 2, row % 2, col // 4, col % 4

    def device(dy=0, dcore=0, dz=0, dx=0):
        return (
            ((y + dy) % 4) * 2 + (core + dcore) % 2,
            ((z + dz) % 4) * 4 + (x + dx) % 4,
        )

    def along(axis, step):
        return device(**{"d" + axis: step % 4})

    coordinate = {"x": x, "y": y, "z": z}
    partner = device(dcore=1)
    forward = (col // 2, (col % 2) * 8 + row)
    backward = (col % 8, 2 * row + col // 8)
    moves = jnp.logical_or(forward[0] != row, forward[1] != col)
    lower_to = (x * 2 + z % 2, y * 4 + 2 * core + z // 2)
    lower_from = (z * 2 + x // 2, (2 * (x % 2) + core) * 4 + y)
    lower_moves = jnp.logical_or(lower_to[0] != row, lower_to[1] != col)

    sent = []
    copies = {}

    def remote(src, dst, send_sem, recv_sem, target):
        return pltpu.make_async_remote_copy(
            src_ref=src, dst_ref=dst, send_sem=send_sem, recv_sem=recv_sem,
            device_id=target, device_id_type=MESH,
        )

    def start(src, dst, send_sem, recv_sem, target):
        copy = remote(src, dst, send_sem, recv_sem, target)
        copy.start()
        sent.append(copy)
        return copy

    barrier = pltpu.get_barrier_semaphore()
    neighbours = [along(a, s) for a in "xyz" for s in (1, 2, 3)] + [partner]
    for target in neighbours:
        pl.semaphore_signal(barrier, inc=1, device_id=target, device_id_type=MESH)

    @pl.when(moves)
    def _():
        for target in (forward, backward):
            pl.semaphore_signal(barrier, inc=1, device_id=target, device_id_type=MESH)

    @pl.when(lower_moves)
    def _():
        for target in (lower_to, lower_from):
            pl.semaphore_signal(barrier, inc=1, device_id=target, device_id_type=MESH)

    load_inv = pltpu.make_async_copy(inverse, inv, local_sem.at[0])
    load_couple = pltpu.make_async_copy(coupling, couple, local_sem.at[1])
    load_diag = pltpu.make_async_copy(diagonal, diag, local_sem.at[2])
    load_inv.start()
    load_couple.start()
    load_diag.start()

    first_row = (row * 16 + col) * PIECE
    block_first = first_row // SN
    block_last = (first_row + PIECE - 1) // SN
    row_at = first_row + lax.broadcasted_iota(jnp.int32, (PIECE, SN), 0)
    in_first = row_at < (block_first + 1) * SN
    for node in range(NODES):
        first_listed = jnp.float32(0)
        last_listed = jnp.float32(0)
        for slot in range(24):
            entry = ancestors[node, slot]
            first_listed = jnp.where(entry == block_first, 1.0, first_listed)
            last_listed = jnp.where(entry == block_last, 1.0, last_listed)
        keep = jnp.where(in_first, first_listed, last_listed)
        masked = jnp.where(keep > 0.5, factor[node].astype(F32), 0.0).astype(BF16)
        own_masked[node] = masked
        lower[node, 0, z, x] = masked[:, :HALF]
        lower[node, 1, z, x] = masked[:, HALF:]

    pl.semaphore_wait(
        barrier, len(neighbours) + 2 * jnp.where(moves, 1, 0) + 2 * jnp.where(lower_moves, 1, 0)
    )

    def piece(node, half, first, second):
        return lower.at[node, half, second, first] if half == 0 else lower.at[node, half, first, second]

    def line(node, half, second):
        return lower.at[node, half, second] if half == 0 else lower.at[node, half, :, second]

    def line_part(node, half, second, part):
        where = pl.ds(2 * part, 2)
        return lower.at[node, half, second, where] if half == 0 else lower.at[node, half, where, second]

    axes = ("xz", "zx")

    def gather_copy(node, half, index, ref, axis, step):
        return start(
            ref, ref, gather_send.at[node, half, index], gather_recv.at[node, half, index], along(axis, step)
        )

    def first_phase(node):
        for half in range(2):
            a = axes[half][0]
            own = piece(node, half, coordinate[a], coordinate[axes[half][1]])
            copies[node, half, 0] = gather_copy(node, half, 0, own, a, 1)
            copies[node, half, 1] = gather_copy(node, half, 1, own, a, 3)

    def first_forward(node):
        for half in range(2):
            a, b = axes[half]
            for index, shift, step, cut in ((0, 3, 1, 0), (1, 1, 3, 128)):
                copies[node, half, index].wait_recv()
                got = piece(node, half, (coordinate[a] + shift) % 4, coordinate[b])
                copies[node, half, index + 2] = gather_copy(
                    node, half, index + 2, got.at[:, pl.ds(cut, 128)], a, step
                )

    def second_phase(node):
        for half in range(2):
            b = axes[half][1]
            copies[node, half, 2].wait_recv()
            copies[node, half, 3].wait_recv()
            own = line(node, half, coordinate[b])
            copies[node, half, 4] = gather_copy(node, half, 4, own, b, 1)
            copies[node, half, 5] = gather_copy(node, half, 5, own, b, 3)

    def second_forward(node):
        for half in range(2):
            b = axes[half][1]
            for index, shift, step, part in ((4, 3, 1, 0), (5, 1, 3, 1)):
                copies[node, half, index].wait_recv()
                got = line_part(node, half, (coordinate[b] + shift) % 4, part)
                copies[node, half, index + 2] = gather_copy(node, half, index + 2, got, b, step)

    def gathered(node, half):
        copies[node, half, 6].wait_recv()
        copies[node, half, 7].wait_recv()

    def multiply(node):
        for half in range(2):
            gathered(node, half)
            right = lower[node, half].reshape(ROWS, HALF)
            for part in range(4):
                rows = pl.ds(part * 192, 192)
                product = dot(inv_high[rows, :], right) + dot(inv_low[rows, :], right)
                partial[node, part, :, :, half * HALF : (half + 1) * HALF] = product.reshape(2, PIECE, HALF)
        copies["trade", node] = start(
            partial.at[node, :, 1 - core], traded.at[node], trade_sem.at[node, 0], trade_sem.at[node, 1], partner
        )

    def chain(later, earlier):
        g = pair_index(later, earlier)

        def body(part, carry):
            value = dot3(traded[earlier, part], couple_high[g], couple_low[g])
            correct[later, part] = value if earlier == 0 else correct[later, part] + value
            return carry

        lax.fori_loop(0, 4, body, 0)

    def reduce_start(node):
        copies["trade", node].wait_recv()
        total = traded[node] + partial[node, :, core]
        if node > 0:
            total = total + correct[node]
        traded[node] = -total
        for way, step in ((0, 1), (1, 3)):
            copies["relay", node, way] = start(
                traded.at[node, pl.ds(2 * way, 2), :, quarter(2)], relay.at[node, way],
                sum_send.at[node, way], sum_recv.at[node, way], along("y", step),
            )

    def quarter(step):
        return pl.ds(pl.multiple_of((y + step) % 4 * QUARTER, QUARTER), QUARTER)

    def reduce_relay(node):
        for way, step in ((0, 1), (1, 3)):
            copies["relay", node, way].wait_recv()
            with_relay, plain = (slice(0, 2), slice(2, 4)) if way == 0 else (slice(2, 4), slice(0, 2))
            outgoing[node, way, with_relay] = traded[node, with_relay, :, quarter(step)] + relay[node, way]
            outgoing[node, way, plain] = traded[node, plain, :, quarter(step)]
            copies["sum", node, way] = start(
                outgoing.at[node, way], arrived.at[node, way],
                sum_send.at[node, 2 + way], sum_recv.at[node, 2 + way], along("y", step),
            )

    def finish(node):
        total = traded[node, :, :, quarter(0)]
        for way in range(2):
            copies["sum", node, way].wait_recv()
            total = total + arrived[node, way]
        solved[node, :, core] = total
        ref = solved.at[node, :, core]
        copies["swap", node] = start(ref, ref, swap_sem.at[node, 0], swap_sem.at[node, 1], partner)

    def rows_start(node):
        at = pl.multiple_of(y * QUARTER, QUARTER)
        where = (node, slice(None), pl.ds(at, QUARTER))
        for step in (1, 2, 3):
            copies["rows", node, step] = start(
                solved.at[node, (y + step) % 4, core], rows_out.at[where],
                rows_send.at[node, step - 1], rows_recv.at[node, step - 1], along("y", step),
            )
        rows_out[where] = solved[node, y, core]

    def columns_copy(node):
        return remote(
            rows_out.at[node], columns_out.at[node], columns_sem.at[node, 0], columns_sem.at[node, 1], forward
        )

    def columns_start(node):
        for step in (1, 2, 3):
            copies["rows", node, step].wait_recv()

        @pl.when(moves)
        def _():
            columns_copy(node).start()

        @pl.when(jnp.logical_not(moves))
        def _():
            columns_out[node] = rows_out[node]

    def columns_wait(node):
        @pl.when(moves)
        def _():
            columns_copy(node).wait()

    def lower_copy():
        return remote(
            own_masked, column_lower.at[:, z % 2, x], lower_sem.at[0], lower_sem.at[1], lower_to
        )

    def lower_start():
        @pl.when(lower_moves)
        def _():
            lower_copy().start()

        @pl.when(jnp.logical_not(lower_moves))
        def _():
            for node in range(NODES):
                column_lower[node, core, y] = own_masked[node]

    def lower_spread():
        @pl.when(lower_moves)
        def _():
            lower_copy().wait()

        ref = column_lower.at[:, core, y]
        for way, step in ((0, 1), (1, 3)):
            copies["spread", way] = start(ref, ref, spread_send.at[way], spread_recv.at[way], along("y", step))

    def lower_relay():
        for way, step in ((0, 1), (1, 3)):
            copies["spread", way].wait_recv()
            ref = column_lower.at[:, core, (y + 4 - step) % 4, :, pl.ds(way * HALF, HALF)]
            copies["spread", 2 + way] = start(
                ref, ref, spread_send.at[2 + way], spread_recv.at[2 + way], along("y", step)
            )

    def lower_both():
        for way in range(2):
            copies["spread", 2 + way].wait_recv()
        ref = column_lower.at[:, core]
        copies["both"] = start(ref, ref, both_sem.at[0], both_sem.at[1], partner)

    def prepare_tilde():
        copies["both"].wait_recv()
        for side_core in range(2):
            for part in range(4):
                rows = pl.ds((side_core * 4 + part) * PIECE, PIECE)
                for node in range(NODES):
                    own = column_lower[node, side_core, part]
                    if node == 0:
                        tilde_high[0, rows, :] = own
                        continue
                    first = column_lower[0, side_core, part]
                    g = pair_index(node, 0)
                    value = own.astype(F32) - (dot(first, couple_high[g]) + dot(first, couple_low[g]))
                    if node == 2:
                        high, low = tilde_high[1, rows, :], tilde_low[1, rows, :]
                        g = pair_index(2, 1)
                        value = value - (
                            dot(high, couple_high[g]) + dot(high, couple_low[g]) + dot(low, couple_high[g])
                        )
                    high, low = split(value)
                    tilde_high[node, rows, :] = high
                    tilde_low[node, rows, :] = low

    def inner_products(later):
        copies["swap", later].wait_recv()
        high, low = split(solved[later].reshape(COLS, QUARTER).T)
        mine = pl.ds(pl.multiple_of(core * HALF, HALF), HALF)
        for earlier in range(later + 1):
            right = tilde_high[earlier, :, mine]
            value = dot(high, right) + dot(low, right)
            if earlier > 0:
                value = value + dot(high, tilde_low[earlier, :, mine])
            for half in range(2):
                cut = value[:, half * QUARTER : (half + 1) * QUARTER]
                inner[half, first_block(later) + earlier] = -cut.reshape(4, 4, 8, QUARTER)

    def down_start(node, level):
        group = slice(first_block(node), first_block(node) + node + 1)
        for half in range(2):
            axis = ("xz", "zx")[half][level]
            for step in (1, 2, 3):
                target = (coordinate[axis] + step) % 4
                if level == 1:
                    src, dst = inner_sum.at[half, group, target], inner_last.at[half, step - 1, group]
                else:
                    src = inner.at[0, group, target] if half == 0 else inner.at[1, group, :, target]
                    dst = inner_recv.at[half, step - 1, group]
                sems = (node, level, half, step - 1)
                copies["down", node, level, half, step] = start(
                    src, dst, down_send.at[sems], down_recv.at[sems], along(axis, step)
                )

    def down_finish(node, level, half):
        group = slice(first_block(node), first_block(node) + node + 1)
        axis = ("xz", "zx")[half][level]
        own = coordinate[axis]
        if level == 1:
            total = inner_sum[half, group, own]
        else:
            total = inner[0, group, own] if half == 0 else inner[1, group, :, own]
        land = (inner_recv, inner_last)[level]
        for step in (1, 2, 3):
            copies["down", node, level, half, step].wait_recv()
            total = total + land[half, step - 1, group]
        return total

    def down_middle(node):
        group = slice(first_block(node), first_block(node) + node + 1)
        for half in range(2):
            inner_sum[half, group] = down_finish(node, 0, half)
        down_start(node, 1)

    def down_last(node):
        for half in range(2):
            total = down_finish(node, 1, half)
            lanes = pl.ds(pl.multiple_of(core * HALF + half * QUARTER, QUARTER), QUARTER)
            for earlier in range(node + 1):
                block = first_block(node) + earlier
                blocks_out[block, core, half, y, x, z] = tail[block, :, lanes] + total[earlier]

    orders = ("yxz", "yzx", "yxz", "zxy", "yzx", "xyz")

    def up_ref(block, level, **other):
        done = orders[block][:level]
        where = [other.get(a, slice(None) if a in done else coordinate[a]) for a in "yxz"]
        return blocks_out.at[(block, core, slice(None), *where)]

    def up_start(block, level):
        axis = orders[block][level]
        ref = up_ref(block, level)
        for step in (1, 2, 3):
            sems = (block, level, step - 1)
            copies["up", block, level, step] = start(ref, ref, up_send.at[sems], up_recv.at[sems], along(axis, step))

    def up_wait(block, level):
        for step in (1, 2, 3):
            copies["up", block, level, step].wait_recv()

    def pair_start(block, step):
        axis = orders[block][2]
        ref = up_ref(block, 2, **{axis: (coordinate[axis] - step) % 4})
        copies["pair", block, step] = start(ref, ref, pair_send.at[block, step], pair_recv.at[block, step], partner)

    def pair_rest(group):
        for step in (1, 3, 2):
            for block in group:
                copies["up", block, 2, step].wait_recv()
                pair_start(block, step)

    finished = pl.ds(pl.multiple_of(y * 128 + x * 32 + z * 8, 8), 8)

    def dot3_t(left, right_high, right_low):
        def across(a, b):
            return lax.dot_general(a, b, (((1,), (1,)), ((), ())), preferred_element_type=F32)

        high, low = split(left)
        return across(high, right_high) + across(high, right_low) + across(low, right_high)

    def split_diag(index):
        high, low = split(diag[index])
        side_high[...] = high
        side_low[...] = low

    def tail_terms():
        taken = []
        for g in range(3):
            side[...] = couple[g].T
            taken.append(side[finished, :])
        first, second, third = taken
        ch, cl = couple_high, couple_low
        mixed = dot3_t(third, ch[0], cl[0])
        stacked = jnp.concatenate([first, second, mixed], axis=0)
        split_diag(0)
        plain = dot3(stacked, side_high[...], side_low[...])
        turned = dot3_t(stacked, side_high[...], side_low[...])
        split_diag(1)
        after = dot3(third, side_high[...], side_low[...])
        after_t = dot3_t(third, side_high[...], side_low[...])
        a1, a2, a3 = plain[0:8], plain[8:16], plain[16:24]
        b1, b2, b3 = turned[0:8], turned[8:16], turned[16:24]
        through = dot3(jnp.concatenate([a1, a2, b3, a3], axis=0), ch[0], cl[0])
        e1, e2, e3, e4 = through[0:8], through[8:16], through[16:24], through[24:32]
        tail[0] = diag[0, finished, :]
        tail[1] = -b1
        tail[2] = diag[1, finished, :] + e1
        tail[3] = b3 - b2
        tail[4] = e2 - after_t - e3
        tail[5] = (
            diag[2, finished, :] + dot3(a2 - b3, ch[1], cl[1]) + dot3(after + e4 - e2, ch[2], cl[2])
        )

    for node in range(NODES):
        first_phase(node)
    first_forward(0)
    second_phase(0)
    first_forward(1)
    first_forward(2)
    lower_start()
    load_inv.wait()
    for block in range(6):
        where = slice(block * 256, (block + 1) * 256)
        high, low = split(inv[where, :].T)
        inv_high[:, where] = high
        inv_low[:, where] = low
    second_forward(0)
    second_phase(1)
    lower_spread()
    load_couple.wait()
    load_diag.wait()
    for g in range(3):
        high, low = split(couple[g])
        couple_high[g] = high
        couple_low[g] = low
    multiply(0)
    second_forward(1)
    second_phase(2)
    lower_relay()
    reduce_start(0)
    chain(1, 0)
    tail_terms()
    multiply(1)
    second_forward(2)
    reduce_relay(0)
    reduce_start(1)
    lower_both()
    chain(2, 0)
    chain(2, 1)
    reduce_relay(1)
    finish(0)
    rows_start(0)
    multiply(2)
    reduce_start(2)
    prepare_tilde()
    inner_products(0)
    reduce_relay(2)
    columns_start(0)
    down_start(0, 0)
    finish(1)
    rows_start(1)
    inner_products(1)
    down_start(1, 0)
    down_middle(0)
    down_middle(1)
    finish(2)
    rows_start(2)
    inner_products(2)
    down_start(2, 0)
    columns_start(1)
    down_last(0)
    down_last(1)
    for block in (0, 1, 2):
        up_start(block, 0)
    down_middle(2)
    columns_start(2)
    for block in (0, 1, 2):
        up_wait(block, 0)
        up_start(block, 1)
    down_last(2)
    for block in (3, 4, 5):
        up_start(block, 0)
    for block in (0, 1, 2):
        up_wait(block, 1)
        up_start(block, 2)
        pair_start(block, 0)
    for block in (3, 4, 5):
        up_wait(block, 0)
        up_start(block, 1)
    for block in (3, 4, 5):
        up_wait(block, 1)
        up_start(block, 2)
        pair_start(block, 0)
    pair_rest((0, 1, 2))
    pair_rest((3, 4, 5))
    for block in range(6):
        for step in range(4):
            copies["pair", block, step].wait_recv()
    for node in range(NODES):
        columns_wait(node)
    for copy in sent:
        copy.wait_send()


def fused(ancestor_inverse, factor, coupling, diagonal_inverse, ancestors):
    vmem = pl.BlockSpec(memory_space=pltpu.VMEM)
    hbm = pl.BlockSpec(memory_space=pl.ANY)
    dma = pltpu.SemaphoreType.DMA
    square = (SN, SN)
    return pl.pallas_call(
        kernel,
        out_shape=(
            jax.ShapeDtypeStruct((NODES, PIECE, SN), F32),
            jax.ShapeDtypeStruct((NODES, PIECE, SN), F32),
            jax.ShapeDtypeStruct((6, 2, 2, 4, 4, 4, 8, QUARTER), F32),
        ),
        in_specs=[hbm, vmem, hbm, hbm, pl.BlockSpec(memory_space=pltpu.SMEM)],
        out_specs=(vmem, vmem, vmem),
        scratch_shapes=[
            pltpu.VMEM((ROWS, COLS), F32),
            pltpu.VMEM((COLS, ROWS), BF16),
            pltpu.VMEM((COLS, ROWS), BF16),
            pltpu.VMEM((NODES, PIECE, SN), BF16),
            pltpu.VMEM((NODES, 2, 4, 4, PIECE, HALF), BF16),
            pltpu.VMEM((NODES, 4, 2, PIECE, SN), F32),
            pltpu.VMEM((NODES, 4, PIECE, SN), F32),
            pltpu.VMEM((NODES, 4, PIECE, SN), F32),
            pltpu.VMEM((NODES, 2, 2, PIECE, QUARTER), F32),
            pltpu.VMEM((NODES, 2, 4, PIECE, QUARTER), F32),
            pltpu.VMEM((NODES, 2, 4, PIECE, QUARTER), F32),
            pltpu.VMEM((NODES, 4, 2, PIECE, QUARTER), F32),
            pltpu.VMEM((3,) + square, F32),
            pltpu.VMEM((3,) + square, BF16),
            pltpu.VMEM((3,) + square, BF16),
            pltpu.VMEM((3,) + square, F32),
            pltpu.VMEM((6, 8, SN), F32),
            pltpu.VMEM(square, F32),
            pltpu.VMEM(square, BF16),
            pltpu.VMEM(square, BF16),
            pltpu.VMEM((NODES, 2, 4, PIECE, SN), BF16),
            pltpu.VMEM((NODES, COLS, SN), BF16),
            pltpu.VMEM((NODES, COLS, SN), BF16),
            pltpu.VMEM((2, 6, 4, 4, 8, QUARTER), F32),
            pltpu.VMEM((2, 3, 6, 4, 8, QUARTER), F32),
            pltpu.VMEM((2, 6, 4, 8, QUARTER), F32),
            pltpu.VMEM((2, 3, 6, 8, QUARTER), F32),
            dma((3,)),
            dma((NODES, 2, 8)),
            dma((NODES, 2, 8)),
            dma((2,)),
            dma((4,)),
            dma((4,)),
            dma((2,)),
            dma((NODES, 2)),
            dma((NODES, 2)),
            dma((NODES, 4)),
            dma((NODES, 4)),
            dma((NODES, 3)),
            dma((NODES, 3)),
            dma((NODES, 2)),
            dma((NODES, 2, 2, 3)),
            dma((NODES, 2, 2, 3)),
            dma((6, 3, 3)),
            dma((6, 3, 3)),
            dma((6, 4)),
            dma((6, 4)),
        ],
        compiler_params=pltpu.CompilerParams(
            collective_id=0, has_side_effects=True, vmem_limit_bytes=63 << 20
        ),
        name="selected_inversion",
    )(ancestor_inverse, factor, coupling, diagonal_inverse, ancestors)


def block_at(step):
    return jnp.where(step > 1, step - 1, step) - jnp.where(step > 4, 1, 0) - jnp.where(step > 6, 1, 0)


def place_at(step):
    turned = jnp.logical_or(step == 2, jnp.logical_or(step == 5, step == 7))
    later = jnp.where(step > 3, 2, jnp.where(step > 0, 1, 0))
    earlier = jnp.where(step == 8, 2, jnp.where(jnp.logical_or(step == 3, step // 2 == 3), 1, 0))
    return turned, jnp.where(turned, earlier, later), jnp.where(turned, later, earlier)


def assemble_kernel(block, rows, columns, out, rows_out, columns_out):
    step = pl.program_id(0)
    turned = place_at(step)[0]

    def lanes(half):
        return block[0, half // 2, half % 2].reshape(SN, QUARTER)

    @pl.when(step == 0)
    def _():
        rows_out[...] = rows[...]
        columns_out[...] = columns[...]

    @pl.when(jnp.logical_not(turned))
    def _():
        for half in range(4):
            out[0, 0, :, half * QUARTER : (half + 1) * QUARTER] = lanes(half)

    @pl.when(turned)
    def _():
        for half in range(4):
            out[0, 0, half * QUARTER : (half + 1) * QUARTER, :] = lanes(half).T


def assemble(blocks, rows, columns):
    whole = pl.BlockSpec(rows.shape, lambda step: (0, 0, 0))
    return pl.pallas_call(
        assemble_kernel,
        out_shape=(
            jax.ShapeDtypeStruct((NODES, NODES, SN, SN), F32),
            jax.ShapeDtypeStruct(rows.shape, F32),
            jax.ShapeDtypeStruct(columns.shape, F32),
        ),
        grid=(9,),
        in_specs=[
            pl.BlockSpec((1, 2, 2, 4, 4, 4, 8, QUARTER), lambda step: (block_at(step),) + (0,) * 7), whole, whole
        ],
        out_specs=(
            pl.BlockSpec((1, 1, SN, SN), lambda step: place_at(step)[1:] + (0, 0)), whole, whole
        ),
        compiler_params=pltpu.CompilerParams(vmem_limit_bytes=60 << 20),
        name="assemble_node_blocks",
    )(blocks, rows, columns)


def local(ancestor_inverse, factor, coupling, diagonal_inverse, ancestors):
    block_rows, block_columns, blocks = fused(
        ancestor_inverse, factor, coupling, diagonal_inverse, ancestors
    )
    node_blocks, block_rows, block_columns = assemble(blocks, block_rows, block_columns)
    return block_columns, block_rows, node_blocks


def solution(mesh):
    placed = (P("row", "col"), P(None, ("row", "col"), None), P(), P(), P())
    return jax.shard_map(
        local,
        mesh=mesh,
        in_specs=placed,
        out_specs=(P(None, ("row", "col"), None), P(None, ("col", "row"), None), P()),
        check_vma=False,
    )
```
